32 devices in a mesh: pairs: 2 (over x), rows: 8 (over z, y), cols: 2 (over core).
Axes of the slice: x: 2, y: 2, z: 4, core: 2. Of those that a mesh axis runs over, the one named last changes fastest.
Arguments:
- left_feat: bfloat16 [32, 512, 256], P(('pairs', 'rows'), 'cols'), parts along dimension 0, may hold values from -6 to 6
- right_feat: bfloat16 [32, 512, 256], P(('pairs', 'rows'), 'cols'), parts along dimension 0, may hold values from -6 to 6
- block_list: int32 [16, 8, 2], P(('pairs', 'rows'), 'cols'), parts along dimension 0, may hold values from 0 to 1, as said below
- block_count: int32 [16, 8], P(('pairs', 'rows'), 'cols'), parts along dimension 0, may hold values from 1 to 2
- spatial_first: bfloat16 [3, 3, 16, 16], replicated, may hold values from -0.75 to 0.75
- spatial_second: bfloat16 [3, 3, 16, 16], replicated, may hold values from -0.75 to 0.75
- disparity_weight: bfloat16 [17, 16], replicated, may hold values from -0.5 to 0.5
Outputs:
- cost: float32 [32, 512, 256], P(('pairs', 'rows'), 'cols'), parts along dimension 0
The draws below stay inside these ranges and needn't reach their ends.
There are 2 independent parts, one for each index of `pairs`. The reference program is written for one: setup_inputs(seed, part) draws one part's arguments, and reference() takes and returns one part's arrays. A program takes and returns all parts, laid end to end along the dimension named above; an argument that names none is the same for every part. Nothing has to cross between parts.
Inputs may be any that keep to these rules, and one draw needn't show every extreme that they name: `block_list`: for each tile the 2 entries are different block numbers; entries in slots at or past the tile's block_count are not listed.
All inputs are finite; a program needn't handle non-finite values.
Results may differ from the reference program's by a relative error of at most 0.0059.
Values may be sent and summed in bfloat16 or wider, within the bound.
A program may use at most 128 MiB of HBM per device.

```python
import jax
import jax.numpy as jnp
from jax import lax

C = 256
G = 16
DB = 128
NBLK = 2
MAXB = 2
TILE = 64
TAPS = 17
TR = 2
BANDS = 8
H = 16
W = 512
TILES = 8
NDISP = 256


def draw_block_list(key, part):
    key = jax.random.fold_in(key, 11)
    scores = jax.random.randint(key, (BANDS, TILES, NBLK), 0, 1 << 20)
    scores = scores * NBLK + jnp.arange(NBLK, dtype=jnp.int32)
    ordering = jnp.argsort(scores, axis=-1, stable=True).astype(jnp.int32)
    return ordering[..., :MAXB]


def draw_block_count(key, part):
    key = jax.random.fold_in(key, 23)
    return jax.random.randint(key, (BANDS, TILES), 1, MAXB + 1).astype(jnp.int32)


def block_scale(rng, dims, cuts, least, largest):
    def one(dim, parts):
        heights = jax.random.uniform(jax.random.fold_in(jax.random.fold_in(rng, 6), dim), (parts,), jnp.float32, least / len(cuts), largest / len(cuts))
        return jnp.repeat(jnp.exp(heights), dims[dim] // parts).reshape((-1,) + (1,) * (len(dims) - dim - 1))

    loudness = one(*cuts[0])
    for cut in cuts[1:]:
        loudness = loudness * one(*cut)
    return loudness


def gaussian(own_key, extent, deviation, bound, shards=(), held_as=jnp.bfloat16):
    loudness = block_scale(own_key, extent, shards, -0.22, 0.18) if shards else 1.0
    array = jax.random.normal(own_key, extent, jnp.float32) * deviation * loudness
    return jnp.minimum(jnp.maximum(array, -bound), bound).astype(held_as)


def setup_inputs(seed: int = 0, part: int = 0) -> dict:
    seeds = jax.random.split(jax.random.key(seed), 8)
    part_splits = jax.random.split(jax.random.fold_in(seeds[7], part), 8)
    return {
        "left_feat": gaussian(part_splits[0], (H, W, C), 1.0, 6.0, ((0, 8), (1, 2))),
        "right_feat": gaussian(part_splits[1], (H, W, C), 1.0, 6.0, ((0, 8), (1, 2))),
        "block_list": draw_block_list(jax.random.fold_in(jax.random.fold_in(seeds[7], part), 71), part),
        "block_count": draw_block_count(jax.random.fold_in(jax.random.fold_in(seeds[7], part), 71), part),
        "spatial_first": gaussian(seeds[4], (3, 3, G, G), (9 * G // 2) ** -0.5, 0.75),
        "spatial_second": gaussian(seeds[5], (3, 3, G, G), (9 * G // 2) ** -0.5, 0.75),
        "disparity_weight": gaussian(seeds[6], (TAPS, G), (TAPS * G // 2) ** -0.5, 0.5),
    }


def skew_band(products):
    pixel_count = products.shape[-2]
    window_len = products.shape[-1]
    block_len = window_len - pixel_count
    leading = products.shape[:-2]
    flattened = products.reshape(leading + (pixel_count * window_len,))
    flattened = jnp.pad(flattened, [(0, 0)] * len(leading) + [(0, pixel_count)])
    skewed = flattened.reshape(leading + (pixel_count, window_len + 1))
    return skewed[..., 1:block_len + 1][..., ::-1]


def group_products(left_piece, right_window):
    row_count, pixel_count, channels = left_piece.shape
    window_len = right_window.shape[1]
    left_groups = left_piece.astype(jnp.float32).reshape(row_count, pixel_count, G, channels // G)
    right_groups = right_window.astype(jnp.float32).reshape(row_count, window_len, G, channels // G)
    products = jnp.einsum("yigc,yjgc->gyij", left_groups, right_groups, precision=lax.Precision.HIGHEST)
    return skew_band(products)


def spatial_same(volume, kernel):
    return lax.conv_general_dilated(volume.astype(jnp.float32), kernel.astype(jnp.float32), (1, 1), ((1, 1), (1, 1)), dimension_numbers=("CHWN", "HWOI", "CHWN"), precision=lax.Precision.HIGHEST)


def disparity_conv(lower_rim, middle, upper_rim, kernel):
    extended = jnp.concatenate([lower_rim, middle, upper_rim], axis=3).astype(jnp.float32)
    weights = kernel.astype(jnp.float32)[None, :, :, None]
    result = lax.conv_general_dilated(extended, weights, (1, 1), "VALID", dimension_numbers=("CHNW", "HWIO", "CHNW"), precision=lax.Precision.HIGHEST)
    return result[0]


def reference(left_feat, right_feat, block_list, block_count, spatial_first, spatial_second, disparity_weight):
    height, breadth, channels = left_feat.shape
    slot_ids = jnp.arange(block_list.shape[2], dtype=jnp.int32)
    live = slot_ids[None, None, :] < block_count[:, :, None]
    block_ids = jnp.arange(NBLK, dtype=jnp.int32)
    hits = (block_list[..., None] == block_ids) & live[..., None]
    active = jnp.any(hits, axis=2).astype(jnp.float32)
    pixel_mask = jnp.repeat(jnp.repeat(active, TR, axis=0), TILE, axis=1)
    right_padded = jnp.pad(right_feat, ((0, 0), (NDISP, 0), (0, 0)))
    corr_scale = (C // G) ** -0.5
    half_taps = TAPS // 2
    lower_rim = jnp.zeros((G, height, breadth, half_taps), jnp.bfloat16)
    current = None
    results = []
    for block_index in range(NBLK):
        def tile_piece(tile_index):
            start = tile_index * TILE
            left_piece = lax.dynamic_slice_in_dim(left_feat, start, TILE, 1)
            right_window = lax.dynamic_slice_in_dim(right_padded, start - block_index * DB - DB + NDISP, TILE + DB, 1)
            return group_products(left_piece, right_window)

        tiles = lax.map(tile_piece, jnp.arange(breadth // TILE, dtype=jnp.int32))
        products = jnp.moveaxis(tiles, 0, 2).reshape(G, height, breadth, DB)
        correlation = (products * corr_scale * pixel_mask[:, :, block_index][None, :, :, None]).astype(jnp.bfloat16)
        first_hidden = jax.nn.relu(spatial_same(correlation, spatial_first)).astype(jnp.bfloat16)
        newest = jax.nn.relu(spatial_same(first_hidden, spatial_second)).astype(jnp.bfloat16)
        if current is not None:
            results.append(disparity_conv(lower_rim, current, newest[..., :half_taps], disparity_weight))
            lower_rim = current[..., DB - half_taps:]
        current = newest
    upper_zero = jnp.zeros((G, height, breadth, half_taps), jnp.bfloat16)
    results.append(disparity_conv(lower_rim, current, upper_zero, disparity_weight))
    return jnp.concatenate(results, axis=-1)
```

```python
import jax
import jax.numpy as jnp
from jax import lax
from jax.experimental import pallas as pl
from jax.experimental.pallas import tpu as pltpu
from jax.sharding import PartitionSpec as P

C = 256
G = 16
CG = C // G
DB = 128
NBLK = 2
ND = DB * NBLK
TILE = 64
TAPS = 17
BLK = 128
RIM = 2
P1 = 6
P2 = 8
PAD = 16
MESH = pl.DeviceIdType.MESH


def window_weights(taps, wide):
    lane = lax.broadcasted_iota(jnp.int32, (G, 4 * BLK), 1)
    group = lax.broadcasted_iota(jnp.int32, (G, 4 * BLK), 0)
    base = jnp.zeros((G, 4 * BLK), jnp.float32)
    for i in range(3):
        for j in range(3):
            pick = (lane == group + (i * wide + j) * G).astype(jnp.float32).astype(jnp.bfloat16)
            base = base + jnp.dot(taps[3 * i + j], pick, preferred_element_type=jnp.float32)
    return base


def kernel(flags, left, right, act, sf, ss, td, out, l32, rt, a_buf, vol, h1, h2, w1, w2, a32):
    ext_rows, ext_cols, _ = left.shape
    strip = ext_cols - 2 * PAD
    out_rows = ext_rows - 2 * RIM
    base = window_weights(sf, P1 + 2)
    for i in range(2):
        for j in range(P1):
            move = (i * (P1 + 2) + j) * G
            piece = pltpu.roll(base, move, 1) if move else base
            at = (i * P1 + j) * G
            w1[at : at + G, :] = piece.astype(jnp.bfloat16)
    base = window_weights(ss, P2 + 2)
    for j in range(P2):
        piece = pltpu.roll(base, j * G, 1) if j else base
        w2[j * G : (j + 1) * G, :] = piece.astype(jnp.bfloat16)
    to = lax.broadcasted_iota(jnp.int32, (P2 * G, P2 * G), 0)
    at = lax.broadcasted_iota(jnp.int32, (P2 * G, P2 * G), 1)
    order = (at == (to % P2) * G + to // P2).astype(jnp.float32).astype(jnp.bfloat16)
    w2[...] = jnp.dot(order, w2[...], preferred_element_type=jnp.float32).astype(jnp.bfloat16)
    tiles = strip // BLK
    back = ND // BLK
    blocks = right.shape[1] // BLK
    chunk = 32
    chan = lax.broadcasted_iota(jnp.int32, (G, C), 1) // CG
    grp = lax.broadcasted_iota(jnp.int32, (G, C), 0)
    diag = (chan == grp).astype(jnp.float32).astype(jnp.bfloat16)

    def fill(y, x_ext, count, slot):
        for i in range(count):
            row = jnp.broadcast_to(l32[pl.ds(x_ext + (PAD - RIM) + i, 1), :], (G, C)).astype(jnp.bfloat16)
            a_buf[slot + i * G : slot + (i + 1) * G, :] = row * diag

    def emit(y, x_ext, prod, i, xi, scale):
        piece = prod[i * G : (i + 1) * G, 1 + xi : 1 + xi + ND]
        vol[y, pl.ds(pl.multiple_of((x_ext + i) * G, G), G), :] = piece * scale

    def row_step(y, carry):
        l32[...] = left[y].astype(jnp.float32)
        for b in range(blocks):
            rt[:, b * BLK : (b + 1) * BLK] = right[y, b * BLK : (b + 1) * BLK, :].T

        for side in range(3):
            a32[side] = act[side, y].astype(jnp.float32)

        def scale_of(side, tile):
            return jnp.broadcast_to(a32[side, pl.ds(tile, 1), :], (G, ND)).astype(jnp.bfloat16)

        def tile_step(t, carry):
            window = rt[:, pl.ds(pl.multiple_of((t + 1) * BLK, BLK), BLK + ND)]
            for half in range(BLK // TILE):
                scale = scale_of(1, t * (BLK // TILE) + half)
                for c in range(TILE // chunk):
                    xi = half * TILE + c * chunk
                    fill(y, RIM + t * BLK + xi, chunk, 0)
                    prod = jnp.dot(
                        a_buf[0 : chunk * G, :], window, preferred_element_type=jnp.float32
                    ).astype(jnp.bfloat16)
                    for i in range(chunk):
                        emit(y, RIM + t * BLK + xi, prod, i, xi + i, scale)
            return carry

        lax.fori_loop(0, tiles, tile_step, 0)
        fill(y, 0, RIM, 0)
        prod = jnp.dot(
            a_buf[0 : RIM * G, :], rt[:, 0 : BLK + ND], preferred_element_type=jnp.float32
        ).astype(jnp.bfloat16)
        scale = scale_of(0, strip // TILE - 1)
        for i in range(RIM):
            emit(y, 0, prod, i, BLK - RIM + i, scale)
        fill(y, RIM + strip, RIM, 0)
        first = (1 + tiles) * BLK
        prod = jnp.dot(
            a_buf[0 : RIM * G, :],
            rt[:, first : first + BLK + ND],
            preferred_element_type=jnp.float32,
        ).astype(jnp.bfloat16)
        scale = scale_of(2, 0)
        for i in range(RIM):
            emit(y, RIM + strip, prod, i, i, scale)
        return carry

    lax.fori_loop(0, ext_rows, row_step, 0)

    def conv1_step(w, carry):
        at = pl.multiple_of(w * (P1 * G), P1 * G)
        for yp in range((out_rows + 2) // 2):
            x = jnp.concatenate(
                [vol[2 * yp + r, pl.ds(at, (P1 + 2) * G), :] for r in range(4)], axis=0
            )
            y = jnp.dot(w1[...], x, preferred_element_type=jnp.float32)
            y = jnp.maximum(y, 0.0).astype(jnp.bfloat16)
            for r in range(2):
                h1[2 * yp + r, pl.ds(at, P1 * G), :] = y[r * P1 * G : (r + 1) * P1 * G, :]
        return carry

    lax.fori_loop(0, (strip + 2) // P1, conv1_step, 0)

    span = (strip + 2) * G

    @pl.when(flags[0] == 0)
    def _():
        h1[0, 0:span, :] = jnp.zeros((span, ND), jnp.bfloat16)

    @pl.when(flags[1] == 0)
    def _():
        h1[out_rows + 1, 0:span, :] = jnp.zeros((span, ND), jnp.bfloat16)

    @pl.when(flags[2] == 0)
    def _():
        h1[:, 0:G, :] = jnp.zeros((out_rows + 2, G, ND), jnp.bfloat16)

    @pl.when(flags[3] == 0)
    def _():
        h1[:, span - G : span, :] = jnp.zeros((out_rows + 2, G, ND), jnp.bfloat16)

    def conv2_step(w, carry):
        for y in range(out_rows):
            halves = []
            for h in range(2):
                at = pl.multiple_of((w * 2 + h) * (P2 * G), P2 * G)
                x = jnp.concatenate(
                    [h1[y + r, pl.ds(at, (P2 + 2) * G), :] for r in range(3)], axis=0
                )
                r = jnp.dot(w2[:, 0 : 3 * (P2 + 2) * G], x, preferred_element_type=jnp.float32)
                halves.append(jnp.maximum(r, 0.0))
            px = pl.multiple_of(y * strip + w * (2 * P2), 2 * P2)
            for g in range(G):
                both = jnp.concatenate([q[g * P2 : (g + 1) * P2] for q in halves], axis=0)
                h2[g, pl.ds(px, 2 * P2), :] = both.astype(jnp.bfloat16)
        return carry

    lax.fori_loop(0, strip // (2 * P2), conv2_step, 0)

    for y in range(out_rows):
        total = None
        for g in range(G):
            part = jnp.dot(
                h2[g, y * strip : (y + 1) * strip, :], td[g], preferred_element_type=jnp.float32
            )
            total = part if total is None else total + part
        out[y] = total


def halo_kernel(dw, left, right, act, lx, rx, ax, td, send, recv, local, row_sem, row_recv):
    rows, strip, _ = left.shape
    band, bands = lax.axis_index("rows"), lax.axis_size("rows")
    col, cols = lax.axis_index("cols"), lax.axis_size("cols")
    own = slice(RIM, RIM + rows)
    r0 = BLK + ND
    has_above, has_below = band > 0, band < bands - 1
    has_prev, has_next = col > 0, col < cols - 1

    barrier = pltpu.get_barrier_semaphore()

    def greet(there, device):
        @pl.when(there)
        def _():
            pl.semaphore_signal(barrier, inc=1, device_id=device, device_id_type=MESH)

    greet(has_above, {"rows": band - 1})
    greet(has_below, {"rows": band + 1})
    greet(has_prev, {"cols": col - 1})
    greet(has_next, {"cols": col + 1})
    sides = (has_above, has_below, has_prev, has_next)
    pl.semaphore_wait(barrier, sum(there.astype(jnp.int32) for there in sides))

    def row_copies(device, first, slot):
        pairs = (
            (left, lx.at[first : first + rows, PAD : PAD + strip]),
            (right, rx.at[first : first + rows, r0 : r0 + strip]),
            (act, ax.at[1, first : first + rows]),
        )
        return [
            pltpu.make_async_remote_copy(
                src_ref=a, dst_ref=b, send_sem=row_sem.at[slot, i], recv_sem=row_recv.at[slot, i],
                device_id=device, device_id_type=MESH,
            )
            for i, (a, b) in enumerate(pairs)
        ]

    def col_copies(forward, part):
        at = slice(part * RIM, part * RIM + RIM)
        if part == 1:
            srcs = (left, right, act)
        else:
            srcs = (
                lx.at[at, PAD : PAD + strip], rx.at[at, r0 : r0 + strip], ax.at[1, at],
            )
        l_src, r_src, a_src = srcs
        if forward:
            pairs = (
                (l_src.at[:, strip - PAD : strip], lx.at[at, 0:PAD]),
                (r_src, rx.at[at, BLK : BLK + strip]),
                (a_src, ax.at[0, at]),
            )
        else:
            pairs = (
                (l_src.at[:, 0:PAD], lx.at[at, PAD + strip : 2 * PAD + strip]),
                (r_src.at[:, 0:PAD], rx.at[at, r0 + strip : r0 + strip + PAD]),
                (a_src, ax.at[2, at]),
            )
        slot = (0 if forward else 3) + part
        device = {"cols": col + 1 if forward else col - 1}
        return [
            pltpu.make_async_remote_copy(
                src_ref=a, dst_ref=b, send_sem=send.at[slot, i], recv_sem=recv.at[slot, i],
                device_id=device, device_id_type=MESH,
            )
            for i, (a, b) in enumerate(pairs)
        ]

    down = row_copies({"rows": band + 1}, 0, 0)
    up = row_copies({"rows": band - 1}, RIM + rows, 1)

    def when(there, action):
        @pl.when(there)
        def _():
            action()

    def start(copies):
        for q in copies:
            q.start()

    def got(copies):
        for q in copies:
            q.wait_recv()

    def sent(copies):
        for q in copies:
            q.wait_send()

    when(has_below, lambda: start(down))
    when(has_above, lambda: start(up))
    when(has_next, lambda: start(col_copies(True, 1)))
    when(has_prev, lambda: start(col_copies(False, 1)))
    mine = [
        pltpu.make_async_copy(left, lx.at[own, PAD : PAD + strip], local.at[0]),
        pltpu.make_async_copy(right, rx.at[own, r0 : r0 + strip], local.at[1]),
        pltpu.make_async_copy(act, ax.at[1, own], local.at[2]),
    ]
    start(mine)

    def zero(ref):
        ref[...] = jnp.zeros(ref.shape, ref.dtype)

    zero(rx.at[:, 0:BLK])
    zero(rx.at[:, r0 + strip + PAD : r0 + strip + BLK])

    def no_prev():
        zero(lx.at[own, 0:PAD])
        zero(rx.at[own, BLK:r0])
        zero(ax.at[0, own])

    def no_next():
        zero(lx.at[own, PAD + strip : 2 * PAD + strip])
        zero(rx.at[own, r0 + strip : r0 + strip + PAD])
        zero(ax.at[2, own])

    when(jnp.logical_not(has_prev), no_prev)
    when(jnp.logical_not(has_next), no_next)

    def no_rows(first):
        def run():
            at = slice(first, first + RIM)
            zero(lx.at[at])
            zero(rx.at[at, BLK : r0 + strip + PAD])
            for side in range(3):
                zero(ax.at[side, at])
        return run

    def halo_rims(first):
        def run():
            at = slice(first, first + RIM)

            def before():
                zero(lx.at[at, 0:PAD])
                zero(rx.at[at, BLK:r0])
                zero(ax.at[0, at])

            def after():
                zero(lx.at[at, PAD + strip : 2 * PAD + strip])
                zero(rx.at[at, r0 + strip : r0 + strip + PAD])
                zero(ax.at[2, at])

            when(jnp.logical_not(has_prev), before)
            when(jnp.logical_not(has_next), after)
        return run

    for there, first in ((has_above, 0), (has_below, RIM + rows)):
        when(jnp.logical_not(there), no_rows(first))
        when(there, halo_rims(first))

    def band_step(e, carry):
        at = e * PAD
        place = (
            ND - 1 + TAPS // 2 - at
            - lax.broadcasted_iota(jnp.int32, (PAD, ND), 0)
            - lax.broadcasted_iota(jnp.int32, (PAD, ND), 1)
        )
        for g in range(G):
            total = jnp.zeros((PAD, ND), jnp.float32)
            for k in range(TAPS):
                total = jnp.where(place == k, dw[k, g], total)
            td[g, pl.ds(pl.multiple_of(at, PAD), PAD), :] = total.astype(jnp.bfloat16)
        return carry

    lax.fori_loop(0, ND // PAD, band_step, 0)

    for there, copies, part in ((has_above, down, 0), (has_below, up, 2)):
        def forward(copies=copies, part=part):
            got(copies)
            when(has_next, lambda: start(col_copies(True, part)))
            when(has_prev, lambda: start(col_copies(False, part)))
        when(there, forward)

    for q in mine:
        q.wait()
    when(has_below, lambda: sent(down))
    when(has_above, lambda: sent(up))
    for there, part in ((None, 1), (has_above, 0), (has_below, 2)):
        def finish(part=part):
            when(has_next, lambda: sent(col_copies(True, part)))
            when(has_prev, lambda: sent(col_copies(False, part)))
            when(has_prev, lambda: got(col_copies(True, part)))
            when(has_next, lambda: got(col_copies(False, part)))
        if there is None:
            finish()
        else:
            when(there, finish)


def body(
    left_feat, right_feat, block_list, block_count, spatial_first, spatial_second, disparity_weight
):
    rows, strip, _ = left_feat.shape
    band, bands = lax.axis_index("rows"), lax.axis_size("rows")
    col, col_count = lax.axis_index("cols"), lax.axis_size("cols")
    if strip != ND or col_count > 2 or rows != RIM:
        raise ValueError("unsupported strip")
    tiles = strip // TILE
    n = rows + 2 * RIM

    live = jnp.arange(block_list.shape[2], dtype=jnp.int32) < block_count[0][:, None]
    lane_block = NBLK - 1 - jnp.arange(ND, dtype=jnp.int32) // DB
    hits = (block_list[0][:, :, None] == lane_block[None, None, :]) & live[:, :, None]
    act = jnp.where(jnp.any(hits, axis=1), CG ** (-0.5), 0.0).astype(jnp.bfloat16)
    act = jnp.broadcast_to(jnp.pad(act, ((0, PAD - tiles), (0, 0)))[None], (rows, PAD, ND))
    flags = jnp.stack([band > 0, band < bands - 1, col > 0, col < col_count - 1]).astype(jnp.int32)

    vmem = pl.BlockSpec(memory_space=pltpu.VMEM)
    smem = pl.BlockSpec(memory_space=pltpu.SMEM)
    right_len = BLK + ND + strip + BLK
    left, right, act, td = pl.pallas_call(
        halo_kernel,
        out_shape=(
            jax.ShapeDtypeStruct((n, strip + 2 * PAD, C), jnp.bfloat16),
            jax.ShapeDtypeStruct((n, right_len, C), jnp.bfloat16),
            jax.ShapeDtypeStruct((3, n, PAD, ND), jnp.bfloat16),
            jax.ShapeDtypeStruct((G, ND, ND), jnp.bfloat16),
        ),
        in_specs=[smem, vmem, vmem, vmem],
        out_specs=(vmem, vmem, vmem, vmem),
        scratch_shapes=[
            pltpu.SemaphoreType.DMA((6, 3)),
            pltpu.SemaphoreType.DMA((6, 3)),
            pltpu.SemaphoreType.DMA((3,)),
            pltpu.SemaphoreType.DMA((2, 3)),
            pltpu.SemaphoreType.DMA((2, 3)),
        ],
        compiler_params=pltpu.CompilerParams(collective_id=0, has_side_effects=True),
        name="halo",
    )(disparity_weight.astype(jnp.float32), left_feat, right_feat, act)

    return pl.pallas_call(
        kernel,
        out_shape=jax.ShapeDtypeStruct((rows, strip, ND), jnp.float32),
        in_specs=[smem] + [vmem] * 6,
        out_specs=vmem,
        scratch_shapes=[
            pltpu.VMEM((strip + 2 * PAD, C), jnp.float32),
            pltpu.VMEM((C, right_len), jnp.bfloat16),
            pltpu.VMEM((32 * G, C), jnp.bfloat16),
            pltpu.VMEM((n, (strip + 2 * RIM) * G, ND), jnp.bfloat16),
            pltpu.VMEM((rows + 2, (strip + 2) * G, ND), jnp.bfloat16),
            pltpu.VMEM((G, rows * strip, ND), jnp.bfloat16),
            pltpu.VMEM((2 * P1 * G, 4 * BLK), jnp.bfloat16),
            pltpu.VMEM((P2 * G, 4 * BLK), jnp.bfloat16),
            pltpu.VMEM((3, PAD, ND), jnp.float32),
        ],
        compiler_params=pltpu.CompilerParams(vmem_limit_bytes=56 * 1024 * 1024),
        name="cost_volume",
    )(
        flags, left, right, act,
        spatial_first.reshape(9, G, G), spatial_second.reshape(9, G, G), td,
    )


def solution(mesh):
    in_specs = (
        P(("pairs", "rows"), "cols", None),
        P(("pairs", "rows"), "cols", None),
        P(("pairs", "rows"), "cols", None),
        P(("pairs", "rows"), "cols"),
        P(),
        P(),
        P(),
    )
    out_specs = P(("pairs", "rows"), "cols", None)
    return jax.shard_map(body, mesh=mesh, in_specs=in_specs, out_specs=out_specs, check_vma=False)
```

```python
import jax
import jax.numpy as jnp
from jax import lax
from jax.experimental import pallas as pl
from jax.experimental.pallas import tpu as pltpu
from jax.sharding import PartitionSpec as P

C = 256
G = 16
CG = C // G
DB = 128
NBLK = 2
ND = DB * NBLK
TILE = 64
TAPS = 17
BLK = 128
RIM = 2
P1 = 6
P2 = 8
PAD = 16
MESH = pl.DeviceIdType.MESH


def window_weights(taps, wide):
    lane = lax.broadcasted_iota(jnp.int32, (G, 4 * BLK), 1)
    group = lax.broadcasted_iota(jnp.int32, (G, 4 * BLK), 0)
    base = jnp.zeros((G, 4 * BLK), jnp.float32)
    for i in range(3):
        for j in range(3):
            pick = (lane == group + (i * wide + j) * G).astype(jnp.float32).astype(jnp.bfloat16)
            base = base + jnp.dot(taps[3 * i + j], pick, preferred_element_type=jnp.float32)
    return base


def kernel(flags, left, right, act, sf, ss, td, out, l32, rt, a_buf, vol, h1, h2, w1, w2, a32):
    ext_rows, ext_cols, _ = left.shape
    strip = ext_cols - 2 * PAD
    out_rows = ext_rows - 2 * RIM
    base = window_weights(sf, P1 + 2)
    for i in range(2):
        for j in range(P1):
            move = (i * (P1 + 2) + j) * G
            piece = pltpu.roll(base, move, 1) if move else base
            at = (i * P1 + j) * G
            w1[at : at + G, :] = piece.astype(jnp.bfloat16)
    base = window_weights(ss, P2 + 2)
    for j in range(P2):
        piece = pltpu.roll(base, j * G, 1) if j else base
        w2[j * G : (j + 1) * G, :] = piece.astype(jnp.bfloat16)
    to = lax.broadcasted_iota(jnp.int32, (P2 * G, P2 * G), 0)
    at = lax.broadcasted_iota(jnp.int32, (P2 * G, P2 * G), 1)
    order = (at == (to % P2) * G + to // P2).astype(jnp.float32).astype(jnp.bfloat16)
    w2[...] = jnp.dot(order, w2[...], preferred_element_type=jnp.float32).astype(jnp.bfloat16)
    tiles = strip // BLK
    back = ND // BLK
    blocks = right.shape[1] // BLK
    chunk = 32
    chan = lax.broadcasted_iota(jnp.int32, (G, C), 1) // CG
    grp = lax.broadcasted_iota(jnp.int32, (G, C), 0)
    diag = (chan == grp).astype(jnp.float32).astype(jnp.bfloat16)

    def fill(y, x_ext, count, slot):
        for i in range(count):
            row = jnp.broadcast_to(l32[pl.ds(x_ext + (PAD - RIM) + i, 1), :], (G, C)).astype(jnp.bfloat16)
            a_buf[slot + i * G : slot + (i + 1) * G, :] = row * diag

    def emit(y, x_ext, prod, i, xi, scale):
        wide = prod[i * G : (i + 1) * G, :]
        piece = pltpu.roll(wide, wide.shape[1] - 1 - xi, 1)[:, :ND].astype(jnp.bfloat16)
        vol[y, pl.ds(pl.multiple_of((x_ext + i) * G, G), G), :] = piece * scale

    def row_step(y, carry):
        l32[...] = left[y].astype(jnp.float32)
        for b in range(blocks):
            rt[:, b * BLK : (b + 1) * BLK] = right[y, b * BLK : (b + 1) * BLK, :].T

        for side in range(3):
            a32[side] = act[side, y].astype(jnp.float32)

        def scale_of(side, tile):
            return jnp.broadcast_to(a32[side, pl.ds(tile, 1), :], (G, ND)).astype(jnp.bfloat16)

        def tile_step(t, carry):
            window = rt[:, pl.ds(pl.multiple_of((t + 1) * BLK, BLK), BLK + ND)]
            for half in range(BLK // TILE):
                scale = scale_of(1, t * (BLK // TILE) + half)
                for c in range(TILE // chunk):
                    xi = half * TILE + c * chunk
                    slot = xi * G
                    fill(y, RIM + t * BLK + xi, chunk, slot)
                    prod = jnp.dot(
                        a_buf[slot : slot + chunk * G, :], window, preferred_element_type=jnp.float32
                    )
                    for i in range(chunk):
                        emit(y, RIM + t * BLK + xi, prod, i, xi + i, scale)
            return carry

        lax.fori_loop(0, tiles, tile_step, 0)
        fill(y, 0, RIM, 0)
        prod = jnp.dot(
            a_buf[0 : RIM * G, :], rt[:, 0 : BLK + ND], preferred_element_type=jnp.float32
        )
        scale = scale_of(0, strip // TILE - 1)
        for i in range(RIM):
            emit(y, 0, prod, i, BLK - RIM + i, scale)
        fill(y, RIM + strip, RIM, 0)
        first = (1 + tiles) * BLK
        prod = jnp.dot(
            a_buf[0 : RIM * G, :],
            rt[:, first : first + BLK + ND],
            preferred_element_type=jnp.float32,
        )
        scale = scale_of(2, 0)
        for i in range(RIM):
            emit(y, RIM + strip, prod, i, i, scale)
        return carry

    lax.fori_loop(0, ext_rows, row_step, 0)

    def conv1_window(w):
        at = w * (P1 * G) if isinstance(w, int) else pl.multiple_of(w * (P1 * G), P1 * G)
        for yp in range((out_rows + 2) // 2):
            x = jnp.concatenate(
                [vol[2 * yp + r, pl.ds(at, (P1 + 2) * G), :] for r in range(4)], axis=0
            )
            y = jnp.dot(w1[...], x, preferred_element_type=jnp.float32)
            y = jnp.maximum(y, 0.0).astype(jnp.bfloat16)
            for r in range(2):
                h1[2 * yp + r, pl.ds(at, P1 * G), :] = y[r * P1 * G : (r + 1) * P1 * G, :]

    def conv1_step(q, carry):
        for i in range(3):
            conv1_window(q * 3 + i)
        return carry

    windows = (strip + 2) // P1
    lax.fori_loop(0, windows // 3, conv1_step, 0)
    for w in range(windows // 3 * 3, windows):
        conv1_window(w)

    span = (strip + 2) * G

    @pl.when(flags[0] == 0)
    def _():
        h1[0, 0:span, :] = jnp.zeros((span, ND), jnp.bfloat16)

    @pl.when(flags[1] == 0)
    def _():
        h1[out_rows + 1, 0:span, :] = jnp.zeros((span, ND), jnp.bfloat16)

    @pl.when(flags[2] == 0)
    def _():
        h1[:, 0:G, :] = jnp.zeros((out_rows + 2, G, ND), jnp.bfloat16)

    @pl.when(flags[3] == 0)
    def _():
        h1[:, span - G : span, :] = jnp.zeros((out_rows + 2, G, ND), jnp.bfloat16)

    def conv2_window(w):
        for y in range(out_rows):
            halves = []
            for h in range(2):
                at = pl.multiple_of((w * 2 + h) * (P2 * G), P2 * G)
                x = jnp.concatenate(
                    [h1[y + r, pl.ds(at, (P2 + 2) * G), :] for r in range(3)], axis=0
                )
                r = jnp.dot(w2[:, 0 : 3 * (P2 + 2) * G], x, preferred_element_type=jnp.float32)
                halves.append(jnp.maximum(r, 0.0))
            px = pl.multiple_of(y * strip + w * (2 * P2), 2 * P2)
            for g in range(G):
                both = jnp.concatenate([q[g * P2 : (g + 1) * P2] for q in halves], axis=0)
                h2[g, pl.ds(px, 2 * P2), :] = both.astype(jnp.bfloat16)

    def conv2_step(q, carry):
        for i in range(2):
            conv2_window(q * 2 + i)
        return carry

    lax.fori_loop(0, strip // (4 * P2), conv2_step, 0)

    for y in range(out_rows):
        total = None
        for g in range(G):
            part = jnp.dot(
                h2[g, y * strip : (y + 1) * strip, :], td[g], preferred_element_type=jnp.float32
            )
            total = part if total is None else total + part
        out[y] = total


def halo_kernel(dw, left, right, act, lx, rx, ax, td, send, recv, local, row_sem, row_recv):
    rows, strip, _ = left.shape
    band, bands = lax.axis_index("rows"), lax.axis_size("rows")
    col, cols = lax.axis_index("cols"), lax.axis_size("cols")
    own = slice(RIM, RIM + rows)
    r0 = BLK + ND
    has_above, has_below = band > 0, band < bands - 1
    has_prev, has_next = col > 0, col < cols - 1

    barrier = pltpu.get_barrier_semaphore()

    def greet(there, device):
        @pl.when(there)
        def _():
            pl.semaphore_signal(barrier, inc=1, device_id=device, device_id_type=MESH)

    greet(has_above, {"rows": band - 1})
    greet(has_below, {"rows": band + 1})
    greet(has_prev, {"cols": col - 1})
    greet(has_next, {"cols": col + 1})
    sides = (has_above, has_below, has_prev, has_next)
    pl.semaphore_wait(barrier, sum(there.astype(jnp.int32) for there in sides))

    def row_copies(device, first, slot):
        pairs = (
            (left, lx.at[first : first + rows, PAD : PAD + strip]),
            (right, rx.at[first : first + rows, r0 : r0 + strip]),
            (act, ax.at[1, first : first + rows]),
        )
        return [
            pltpu.make_async_remote_copy(
                src_ref=a, dst_ref=b, send_sem=row_sem.at[slot, i], recv_sem=row_recv.at[slot, i],
                device_id=device, device_id_type=MESH,
            )
            for i, (a, b) in enumerate(pairs)
        ]

    def col_copies(forward, part):
        at = slice(part * RIM, part * RIM + RIM)
        if part == 1:
            srcs = (left, right, act)
        else:
            srcs = (
                lx.at[at, PAD : PAD + strip], rx.at[at, r0 : r0 + strip], ax.at[1, at],
            )
        l_src, r_src, a_src = srcs
        if forward:
            pairs = (
                (l_src.at[:, strip - PAD : strip], lx.at[at, 0:PAD]),
                (r_src, rx.at[at, BLK : BLK + strip]),
                (a_src, ax.at[0, at]),
            )
        else:
            pairs = (
                (l_src.at[:, 0:PAD], lx.at[at, PAD + strip : 2 * PAD + strip]),
                (r_src.at[:, 0:PAD], rx.at[at, r0 + strip : r0 + strip + PAD]),
                (a_src, ax.at[2, at]),
            )
        slot = (0 if forward else 3) + part
        device = {"cols": col + 1 if forward else col - 1}
        return [
            pltpu.make_async_remote_copy(
                src_ref=a, dst_ref=b, send_sem=send.at[slot, i], recv_sem=recv.at[slot, i],
                device_id=device, device_id_type=MESH,
            )
            for i, (a, b) in enumerate(pairs)
        ]

    down = row_copies({"rows": band + 1}, 0, 0)
    up = row_copies({"rows": band - 1}, RIM + rows, 1)

    def when(there, action):
        @pl.when(there)
        def _():
            action()

    def start(copies):
        for q in copies:
            q.start()

    def got(copies):
        for q in copies:
            q.wait_recv()

    def sent(copies):
        for q in copies:
            q.wait_send()

    when(has_below, lambda: start(down))
    when(has_above, lambda: start(up))
    when(has_next, lambda: start(col_copies(True, 1)))
    when(has_prev, lambda: start(col_copies(False, 1)))
    mine = [
        pltpu.make_async_copy(left, lx.at[own, PAD : PAD + strip], local.at[0]),
        pltpu.make_async_copy(right, rx.at[own, r0 : r0 + strip], local.at[1]),
        pltpu.make_async_copy(act, ax.at[1, own], local.at[2]),
    ]
    start(mine)

    def zero(ref):
        ref[...] = jnp.zeros(ref.shape, ref.dtype)

    zero(rx.at[:, 0:BLK])
    zero(rx.at[:, r0 + strip + PAD : r0 + strip + BLK])

    def no_prev():
        zero(lx.at[own, 0:PAD])
        zero(rx.at[own, BLK:r0])
        zero(ax.at[0, own])

    def no_next():
        zero(lx.at[own, PAD + strip : 2 * PAD + strip])
        zero(rx.at[own, r0 + strip : r0 + strip + PAD])
        zero(ax.at[2, own])

    when(jnp.logical_not(has_prev), no_prev)
    when(jnp.logical_not(has_next), no_next)

    def no_rows(first):
        def run():
            at = slice(first, first + RIM)
            zero(lx.at[at])
            zero(rx.at[at, BLK : r0 + strip + PAD])
            for side in range(3):
                zero(ax.at[side, at])
        return run

    def halo_rims(first):
        def run():
            at = slice(first, first + RIM)

            def before():
                zero(lx.at[at, 0:PAD])
                zero(rx.at[at, BLK:r0])
                zero(ax.at[0, at])

            def after():
                zero(lx.at[at, PAD + strip : 2 * PAD + strip])
                zero(rx.at[at, r0 + strip : r0 + strip + PAD])
                zero(ax.at[2, at])

            when(jnp.logical_not(has_prev), before)
            when(jnp.logical_not(has_next), after)
        return run

    for there, first in ((has_above, 0), (has_below, RIM + rows)):
        when(jnp.logical_not(there), no_rows(first))
        when(there, halo_rims(first))

    def band_steps(lane, first, last):
        def step(e, carry):
            at = e * PAD
            place = (
                ND - 1 + TAPS // 2 - lane - at
                - lax.broadcasted_iota(jnp.int32, (PAD, BLK), 0)
                - lax.broadcasted_iota(jnp.int32, (PAD, BLK), 1)
            )
            for g in range(G):
                total = jnp.zeros((PAD, BLK), jnp.float32)
                for k in range(TAPS):
                    total = jnp.where(place == k, dw[k, g], total)
                td[g, pl.ds(pl.multiple_of(at, PAD), PAD), lane : lane + BLK] = total.astype(
                    jnp.bfloat16
                )
            return carry

        lax.fori_loop(first, last, step, 0)

    half = BLK // PAD
    td[:, 0 : BLK - PAD, 0:BLK] = jnp.zeros((G, BLK - PAD, BLK), jnp.bfloat16)
    td[:, BLK + PAD : ND, BLK:ND] = jnp.zeros((G, BLK - PAD, BLK), jnp.bfloat16)
    band_steps(0, half - 1, 2 * half)
    band_steps(BLK, 0, half + 1)

    for there, copies, part in ((has_above, down, 0), (has_below, up, 2)):
        def forward(copies=copies, part=part):
            got(copies)
            when(has_next, lambda: start(col_copies(True, part)))
            when(has_prev, lambda: start(col_copies(False, part)))
        when(there, forward)

    for q in mine:
        q.wait()
    when(has_below, lambda: sent(down))
    when(has_above, lambda: sent(up))
    for there, part in ((None, 1), (has_above, 0), (has_below, 2)):
        def finish(part=part):
            when(has_next, lambda: sent(col_copies(True, part)))
            when(has_prev, lambda: sent(col_copies(False, part)))
            when(has_prev, lambda: got(col_copies(True, part)))
            when(has_next, lambda: got(col_copies(False, part)))
        if there is None:
            finish()
        else:
            when(there, finish)


def body(
    left_feat, right_feat, block_list, block_count, spatial_first, spatial_second, disparity_weight
):
    rows, strip, _ = left_feat.shape
    band, bands = lax.axis_index("rows"), lax.axis_size("rows")
    col, col_count = lax.axis_index("cols"), lax.axis_size("cols")
    if strip != ND or col_count > 2 or rows != RIM:
        raise ValueError("unsupported strip")
    tiles = strip // TILE
    n = rows + 2 * RIM

    live = jnp.arange(block_list.shape[2], dtype=jnp.int32) < block_count[0][:, None]
    lane_block = NBLK - 1 - jnp.arange(ND, dtype=jnp.int32) // DB
    hits = (block_list[0][:, :, None] == lane_block[None, None, :]) & live[:, :, None]
    act = jnp.where(jnp.any(hits, axis=1), CG ** (-0.5), 0.0).astype(jnp.bfloat16)
    act = jnp.broadcast_to(jnp.pad(act, ((0, PAD - tiles), (0, 0)))[None], (rows, PAD, ND))
    flags = jnp.stack([band > 0, band < bands - 1, col > 0, col < col_count - 1]).astype(jnp.int32)

    vmem = pl.BlockSpec(memory_space=pltpu.VMEM)
    smem = pl.BlockSpec(memory_space=pltpu.SMEM)
    right_len = BLK + ND + strip + BLK
    left, right, act, td = pl.pallas_call(
        halo_kernel,
        out_shape=(
            jax.ShapeDtypeStruct((n, strip + 2 * PAD, C), jnp.bfloat16),
            jax.ShapeDtypeStruct((n, right_len, C), jnp.bfloat16),
            jax.ShapeDtypeStruct((3, n, PAD, ND), jnp.bfloat16),
            jax.ShapeDtypeStruct((G, ND, ND), jnp.bfloat16),
        ),
        in_specs=[smem, vmem, vmem, vmem],
        out_specs=(vmem, vmem, vmem, vmem),
        scratch_shapes=[
            pltpu.SemaphoreType.DMA((6, 3)),
            pltpu.SemaphoreType.DMA((6, 3)),
            pltpu.SemaphoreType.DMA((3,)),
            pltpu.SemaphoreType.DMA((2, 3)),
            pltpu.SemaphoreType.DMA((2, 3)),
        ],
        compiler_params=pltpu.CompilerParams(collective_id=0, has_side_effects=True),
        name="halo",
    )(disparity_weight.astype(jnp.float32), left_feat, right_feat, act)

    return pl.pallas_call(
        kernel,
        out_shape=jax.ShapeDtypeStruct((rows, strip, ND), jnp.float32),
        in_specs=[smem] + [vmem] * 6,
        out_specs=vmem,
        scratch_shapes=[
            pltpu.VMEM((strip + 2 * PAD, C), jnp.float32),
            pltpu.VMEM((C, right_len), jnp.bfloat16),
            pltpu.VMEM((BLK * G, C), jnp.bfloat16),
            pltpu.VMEM((n, (strip + 2 * RIM) * G, ND), jnp.bfloat16),
            pltpu.VMEM((rows + 2, (strip + 2) * G, ND), jnp.bfloat16),
            pltpu.VMEM((G, rows * strip, ND), jnp.bfloat16),
            pltpu.VMEM((2 * P1 * G, 4 * BLK), jnp.bfloat16),
            pltpu.VMEM((P2 * G, 4 * BLK), jnp.bfloat16),
            pltpu.VMEM((3, PAD, ND), jnp.float32),
        ],
        compiler_params=pltpu.CompilerParams(vmem_limit_bytes=56 * 1024 * 1024),
        name="cost_volume",
    )(
        flags, left, right, act,
        spatial_first.reshape(9, G, G), spatial_second.reshape(9, G, G), td,
    )


def solution(mesh):
    in_specs = (
        P(("pairs", "rows"), "cols", None),
        P(("pairs", "rows"), "cols", None),
        P(("pairs", "rows"), "cols", None),
        P(("pairs", "rows"), "cols"),
        P(),
        P(),
        P(),
    )
    out_specs = P(("pairs", "rows"), "cols", None)
    return jax.shard_map(body, mesh=mesh, in_specs=in_specs, out_specs=out_specs, check_vma=False)
```

```python
import jax
import jax.numpy as jnp
from jax import lax
from jax.experimental import pallas as pl
from jax.experimental.pallas import tpu as pltpu
from jax.sharding import PartitionSpec as P

C = 256
G = 16
CG = C // G
DB = 128
NBLK = 2
ND = DB * NBLK
TILE = 64
TAPS = 17
BLK = 128
RIM = 2
P1 = 6
P2 = 8
PAD = 16
MESH = pl.DeviceIdType.MESH


def window_weights(taps, wide):
    lane = lax.broadcasted_iota(jnp.int32, (G, 4 * BLK), 1)
    group = lax.broadcasted_iota(jnp.int32, (G, 4 * BLK), 0)
    base = jnp.zeros((G, 4 * BLK), jnp.float32)
    for i in range(3):
        for j in range(3):
            pick = (lane == group + (i * wide + j) * G).astype(jnp.float32).astype(jnp.bfloat16)
            base = base + jnp.dot(taps[3 * i + j], pick, preferred_element_type=jnp.float32)
    return base


def weights(sf, ss, w1, w2):
    base = window_weights(sf, P1 + 2)
    for i in range(2):
        for j in range(P1):
            move = (i * (P1 + 2) + j) * G
            piece = pltpu.roll(base, move, 1) if move else base
            at = (i * P1 + j) * G
            w1[at : at + G, :] = piece.astype(jnp.bfloat16)
    base = window_weights(ss, P2 + 2)
    for j in range(P2):
        piece = pltpu.roll(base, j * G, 1) if j else base
        w2[j * G : (j + 1) * G, :] = piece.astype(jnp.bfloat16)
    to = lax.broadcasted_iota(jnp.int32, (P2 * G, P2 * G), 0)
    at = lax.broadcasted_iota(jnp.int32, (P2 * G, P2 * G), 1)
    order = (at == (to % P2) * G + to // P2).astype(jnp.float32).astype(jnp.bfloat16)
    w2[...] = jnp.dot(order, w2[...], preferred_element_type=jnp.float32).astype(jnp.bfloat16)


def correlate(steps, row_of, left, right, act, l32, rt, a_buf, vol, a32):
    strip = left.shape[1] - 2 * PAD
    tiles = strip // BLK
    blocks = right.shape[1] // BLK
    chunk = 32
    chan = lax.broadcasted_iota(jnp.int32, (G, C), 1) // CG
    grp = lax.broadcasted_iota(jnp.int32, (G, C), 0)
    diag = (chan == grp).astype(jnp.float32).astype(jnp.bfloat16)

    def fill(y, x_ext, count, slot):
        for i in range(count):
            row = jnp.broadcast_to(l32[pl.ds(x_ext + (PAD - RIM) + i, 1), :], (G, C)).astype(jnp.bfloat16)
            a_buf[slot + i * G : slot + (i + 1) * G, :] = row * diag

    def emit(y, x_ext, prod, i, xi, scale):
        wide = prod[i * G : (i + 1) * G, :]
        piece = pltpu.roll(wide, wide.shape[1] - 1 - xi, 1)[:, :ND].astype(jnp.bfloat16)
        vol[y, pl.ds(pl.multiple_of((x_ext + i) * G, G), G), :] = piece * scale

    def row_step(step, carry):
        y = row_of(step)
        l32[...] = left[y].astype(jnp.float32)
        for b in range(blocks):
            rt[:, b * BLK : (b + 1) * BLK] = right[y, b * BLK : (b + 1) * BLK, :].T

        for side in range(3):
            a32[side] = act[side, y].astype(jnp.float32)

        def scale_of(side, tile):
            return jnp.broadcast_to(a32[side, pl.ds(tile, 1), :], (G, ND)).astype(jnp.bfloat16)

        def tile_step(t, carry):
            window = rt[:, pl.ds(pl.multiple_of((t + 1) * BLK, BLK), BLK + ND)]
            for half in range(BLK // TILE):
                scale = scale_of(1, t * (BLK // TILE) + half)
                for c in range(TILE // chunk):
                    xi = half * TILE + c * chunk
                    slot = xi * G
                    fill(y, RIM + t * BLK + xi, chunk, slot)
                    prod = jnp.dot(
                        a_buf[slot : slot + chunk * G, :], window, preferred_element_type=jnp.float32
                    )
                    for i in range(chunk):
                        emit(y, RIM + t * BLK + xi, prod, i, xi + i, scale)
            return carry

        lax.fori_loop(0, tiles, tile_step, 0)
        fill(y, 0, RIM, 0)
        prod = jnp.dot(
            a_buf[0 : RIM * G, :], rt[:, 0 : BLK + ND], preferred_element_type=jnp.float32
        )
        scale = scale_of(0, strip // TILE - 1)
        for i in range(RIM):
            emit(y, 0, prod, i, BLK - RIM + i, scale)
        fill(y, RIM + strip, RIM, 0)
        first = (1 + tiles) * BLK
        prod = jnp.dot(
            a_buf[0 : RIM * G, :],
            rt[:, first : first + BLK + ND],
            preferred_element_type=jnp.float32,
        )
        scale = scale_of(2, 0)
        for i in range(RIM):
            emit(y, RIM + strip, prod, i, i, scale)
        return carry

    lax.fori_loop(0, steps, row_step, 0)


def convolve(sides, td, out, vol, h1, h2, w1, w2):
    out_rows, strip, _ = out.shape

    def conv1_window(w):
        at = w * (P1 * G) if isinstance(w, int) else pl.multiple_of(w * (P1 * G), P1 * G)
        for yp in range((out_rows + 2) // 2):
            x = jnp.concatenate(
                [vol[2 * yp + r, pl.ds(at, (P1 + 2) * G), :] for r in range(4)], axis=0
            )
            y = jnp.dot(w1[...], x, preferred_element_type=jnp.float32)
            y = jnp.maximum(y, 0.0).astype(jnp.bfloat16)
            for r in range(2):
                h1[2 * yp + r, pl.ds(at, P1 * G), :] = y[r * P1 * G : (r + 1) * P1 * G, :]

    def conv1_step(q, carry):
        for i in range(3):
            conv1_window(q * 3 + i)
        return carry

    windows = (strip + 2) // P1
    lax.fori_loop(0, windows // 3, conv1_step, 0)
    for w in range(windows // 3 * 3, windows):
        conv1_window(w)

    span = (strip + 2) * G

    @pl.when(jnp.logical_not(sides[0]))
    def _():
        h1[0, 0:span, :] = jnp.zeros((span, ND), jnp.bfloat16)

    @pl.when(jnp.logical_not(sides[1]))
    def _():
        h1[out_rows + 1, 0:span, :] = jnp.zeros((span, ND), jnp.bfloat16)

    @pl.when(jnp.logical_not(sides[2]))
    def _():
        h1[:, 0:G, :] = jnp.zeros((out_rows + 2, G, ND), jnp.bfloat16)

    @pl.when(jnp.logical_not(sides[3]))
    def _():
        h1[:, span - G : span, :] = jnp.zeros((out_rows + 2, G, ND), jnp.bfloat16)

    def conv2_window(w):
        for y in range(out_rows):
            halves = []
            for h in range(2):
                at = pl.multiple_of((w * 2 + h) * (P2 * G), P2 * G)
                x = jnp.concatenate(
                    [h1[y + r, pl.ds(at, (P2 + 2) * G), :] for r in range(3)], axis=0
                )
                r = jnp.dot(w2[:, 0 : 3 * (P2 + 2) * G], x, preferred_element_type=jnp.float32)
                halves.append(jnp.maximum(r, 0.0))
            px = pl.multiple_of(y * strip + w * (2 * P2), 2 * P2)
            for g in range(G):
                both = jnp.concatenate([q[g * P2 : (g + 1) * P2] for q in halves], axis=0)
                h2[g, pl.ds(px, 2 * P2), :] = both.astype(jnp.bfloat16)

    def conv2_step(q, carry):
        for i in range(2):
            conv2_window(q * 2 + i)
        return carry

    lax.fori_loop(0, strip // (4 * P2), conv2_step, 0)

    for y in range(out_rows):
        total = None
        for g in range(G):
            part = jnp.dot(
                h2[g, y * strip : (y + 1) * strip, :], td[g], preferred_element_type=jnp.float32
            )
            total = part if total is None else total + part
        out[y] = total


def kernel(
    dw, left, right, act, sf, ss, out, lx, rx, ax, td, l32, rt, a_buf, vol, h1, h2, w1, w2, a32,
    send, recv, local, row_sem, row_recv,
):
    rows, strip, _ = left.shape
    band, bands = lax.axis_index("rows"), lax.axis_size("rows")
    col, cols = lax.axis_index("cols"), lax.axis_size("cols")
    own = slice(RIM, RIM + rows)
    r0 = BLK + ND
    has_above, has_below = band > 0, band < bands - 1
    has_prev, has_next = col > 0, col < cols - 1

    barrier = pltpu.get_barrier_semaphore()

    def greet(there, device):
        @pl.when(there)
        def _():
            pl.semaphore_signal(barrier, inc=1, device_id=device, device_id_type=MESH)

    greet(has_above, {"rows": band - 1})
    greet(has_below, {"rows": band + 1})
    greet(has_prev, {"cols": col - 1})
    greet(has_next, {"cols": col + 1})
    sides = (has_above, has_below, has_prev, has_next)
    pl.semaphore_wait(barrier, sum(there.astype(jnp.int32) for there in sides))

    def row_copies(device, first, slot):
        pairs = (
            (left, lx.at[first : first + rows, PAD : PAD + strip]),
            (right, rx.at[first : first + rows, r0 : r0 + strip]),
            (act, ax.at[1, first : first + rows]),
        )
        return [
            pltpu.make_async_remote_copy(
                src_ref=a, dst_ref=b, send_sem=row_sem.at[slot, i], recv_sem=row_recv.at[slot, i],
                device_id=device, device_id_type=MESH,
            )
            for i, (a, b) in enumerate(pairs)
        ]

    def col_copies(forward, part):
        at = slice(part * RIM, part * RIM + RIM)
        if part == 1:
            srcs = (left, right, act)
        else:
            srcs = (
                lx.at[at, PAD : PAD + strip], rx.at[at, r0 : r0 + strip], ax.at[1, at],
            )
        l_src, r_src, a_src = srcs
        if forward:
            pairs = (
                (l_src.at[:, strip - PAD : strip], lx.at[at, 0:PAD]),
                (r_src, rx.at[at, BLK : BLK + strip]),
                (a_src, ax.at[0, at]),
            )
        else:
            pairs = (
                (l_src.at[:, 0:PAD], lx.at[at, PAD + strip : 2 * PAD + strip]),
                (r_src.at[:, 0:PAD], rx.at[at, r0 + strip : r0 + strip + PAD]),
                (a_src, ax.at[2, at]),
            )
        slot = (0 if forward else 3) + part
        device = {"cols": col + 1 if forward else col - 1}
        return [
            pltpu.make_async_remote_copy(
                src_ref=a, dst_ref=b, send_sem=send.at[slot, i], recv_sem=recv.at[slot, i],
                device_id=device, device_id_type=MESH,
            )
            for i, (a, b) in enumerate(pairs)
        ]

    down = row_copies({"rows": band + 1}, 0, 0)
    up = row_copies({"rows": band - 1}, RIM + rows, 1)

    def when(there, action):
        @pl.when(there)
        def _():
            action()

    def start(copies):
        for q in copies:
            q.start()

    def got(copies):
        for q in copies:
            q.wait_recv()

    def sent(copies):
        for q in copies:
            q.wait_send()

    when(has_below, lambda: start(down))
    when(has_above, lambda: start(up))
    when(has_next, lambda: start(col_copies(True, 1)))
    when(has_prev, lambda: start(col_copies(False, 1)))
    mine = [
        pltpu.make_async_copy(left, lx.at[own, PAD : PAD + strip], local.at[0]),
        pltpu.make_async_copy(right, rx.at[own, r0 : r0 + strip], local.at[1]),
        pltpu.make_async_copy(act, ax.at[1, own], local.at[2]),
    ]
    start(mine)

    def zero(ref):
        ref[...] = jnp.zeros(ref.shape, ref.dtype)

    zero(rx.at[:, 0:BLK])
    zero(rx.at[:, r0 + strip + PAD : r0 + strip + BLK])

    def no_prev():
        zero(lx.at[own, 0:PAD])
        zero(rx.at[own, BLK:r0])
        zero(ax.at[0, own])

    def no_next():
        zero(lx.at[own, PAD + strip : 2 * PAD + strip])
        zero(rx.at[own, r0 + strip : r0 + strip + PAD])
        zero(ax.at[2, own])

    when(jnp.logical_not(has_prev), no_prev)
    when(jnp.logical_not(has_next), no_next)

    def no_rows(first):
        def run():
            at = slice(first, first + RIM)
            zero(lx.at[at])
            zero(rx.at[at, BLK : r0 + strip + PAD])
            for side in range(3):
                zero(ax.at[side, at])
        return run

    def halo_rims(first):
        def run():
            at = slice(first, first + RIM)

            def before():
                zero(lx.at[at, 0:PAD])
                zero(rx.at[at, BLK:r0])
                zero(ax.at[0, at])

            def after():
                zero(lx.at[at, PAD + strip : 2 * PAD + strip])
                zero(rx.at[at, r0 + strip : r0 + strip + PAD])
                zero(ax.at[2, at])

            when(jnp.logical_not(has_prev), before)
            when(jnp.logical_not(has_next), after)
        return run

    for there, first in ((has_above, 0), (has_below, RIM + rows)):
        when(jnp.logical_not(there), no_rows(first))
        when(there, halo_rims(first))

    def band_steps(lane, first, last):
        def step(e, carry):
            at = e * PAD
            place = (
                ND - 1 + TAPS // 2 - lane - at
                - lax.broadcasted_iota(jnp.int32, (PAD, BLK), 0)
                - lax.broadcasted_iota(jnp.int32, (PAD, BLK), 1)
            )
            for g in range(G):
                total = jnp.zeros((PAD, BLK), jnp.float32)
                for k in range(TAPS):
                    total = jnp.where(place == k, dw[k, g], total)
                td[g, pl.ds(pl.multiple_of(at, PAD), PAD), lane : lane + BLK] = total.astype(
                    jnp.bfloat16
                )
            return carry

        lax.fori_loop(first, last, step, 0)

    half = BLK // PAD
    td[:, 0 : BLK - PAD, 0:BLK] = jnp.zeros((G, BLK - PAD, BLK), jnp.bfloat16)
    td[:, BLK + PAD : ND, BLK:ND] = jnp.zeros((G, BLK - PAD, BLK), jnp.bfloat16)
    band_steps(0, half - 1, 2 * half)
    band_steps(BLK, 0, half + 1)

    weights(sf, ss, w1, w2)

    def arrived(part):
        when(has_prev, lambda: got(col_copies(True, part)))
        when(has_next, lambda: got(col_copies(False, part)))

    def left_off(part):
        when(has_next, lambda: sent(col_copies(True, part)))
        when(has_prev, lambda: sent(col_copies(False, part)))

    for q in mine:
        q.wait()
    arrived(1)
    work = (lx, rx, ax, l32, rt, a_buf, vol, a32)
    correlate(rows, lambda i: i + RIM, *work)

    halves = ((has_above, down, 0), (has_below, up, 2))
    for there, copies, part in halves:
        def forward(copies=copies, part=part):
            got(copies)
            when(has_next, lambda: start(col_copies(True, part)))
            when(has_prev, lambda: start(col_copies(False, part)))
        when(there, forward)
    for there, copies, part in halves:
        when(there, lambda part=part: arrived(part))
    correlate(2 * RIM, lambda i: i + (i // RIM) * rows, *work)

    when(has_below, lambda: sent(down))
    when(has_above, lambda: sent(up))
    left_off(1)
    for there, copies, part in halves:
        when(there, lambda part=part: left_off(part))
    convolve(sides, td, out, vol, h1, h2, w1, w2)


def body(
    left_feat, right_feat, block_list, block_count, spatial_first, spatial_second, disparity_weight
):
    rows, strip, _ = left_feat.shape
    if strip != ND or lax.axis_size("cols") > 2 or rows != RIM:
        raise ValueError("unsupported strip")
    tiles = strip // TILE
    n = rows + 2 * RIM

    live = jnp.arange(block_list.shape[2], dtype=jnp.int32) < block_count[0][:, None]
    lane_block = NBLK - 1 - jnp.arange(ND, dtype=jnp.int32) // DB
    hits = (block_list[0][:, :, None] == lane_block[None, None, :]) & live[:, :, None]
    act = jnp.where(jnp.any(hits, axis=1), CG ** (-0.5), 0.0).astype(jnp.bfloat16)
    act = jnp.broadcast_to(jnp.pad(act, ((0, PAD - tiles), (0, 0)))[None], (rows, PAD, ND))

    vmem = pl.BlockSpec(memory_space=pltpu.VMEM)
    smem = pl.BlockSpec(memory_space=pltpu.SMEM)
    right_len = BLK + ND + strip + BLK
    return pl.pallas_call(
        kernel,
        out_shape=jax.ShapeDtypeStruct((rows, strip, ND), jnp.float32),
        in_specs=[smem] + [vmem] * 5,
        out_specs=vmem,
        scratch_shapes=[
            pltpu.VMEM((n, strip + 2 * PAD, C), jnp.bfloat16),
            pltpu.VMEM((n, right_len, C), jnp.bfloat16),
            pltpu.VMEM((3, n, PAD, ND), jnp.bfloat16),
            pltpu.VMEM((G, ND, ND), jnp.bfloat16),
            pltpu.VMEM((strip + 2 * PAD, C), jnp.float32),
            pltpu.VMEM((C, right_len), jnp.bfloat16),
            pltpu.VMEM((BLK * G, C), jnp.bfloat16),
            pltpu.VMEM((n, (strip + 2 * RIM) * G, ND), jnp.bfloat16),
            pltpu.VMEM((rows + 2, (strip + 2) * G, ND), jnp.bfloat16),
            pltpu.VMEM((G, rows * strip, ND), jnp.bfloat16),
            pltpu.VMEM((2 * P1 * G, 4 * BLK), jnp.bfloat16),
            pltpu.VMEM((P2 * G, 4 * BLK), jnp.bfloat16),
            pltpu.VMEM((3, PAD, ND), jnp.float32),
            pltpu.SemaphoreType.DMA((6, 3)),
            pltpu.SemaphoreType.DMA((6, 3)),
            pltpu.SemaphoreType.DMA((3,)),
            pltpu.SemaphoreType.DMA((2, 3)),
            pltpu.SemaphoreType.DMA((2, 3)),
        ],
        compiler_params=pltpu.CompilerParams(
            collective_id=0, has_side_effects=True, vmem_limit_bytes=56 * 1024 * 1024
        ),
        name="cost_volume",
    )(
        disparity_weight.astype(jnp.float32), left_feat, right_feat, act,
        spatial_first.reshape(9, G, G), spatial_second.reshape(9, G, G),
    )


def solution(mesh):
    in_specs = (
        P(("pairs", "rows"), "cols", None),
        P(("pairs", "rows"), "cols", None),
        P(("pairs", "rows"), "cols", None),
        P(("pairs", "rows"), "cols"),
        P(),
        P(),
        P(),
    )
    out_specs = P(("pairs", "rows"), "cols", None)
    return jax.shard_map(body, mesh=mesh, in_specs=in_specs, out_specs=out_specs, check_vma=False)
```

```python
import jax
import jax.numpy as jnp
from jax import lax
from jax.experimental import pallas as pl
from jax.experimental.pallas import tpu as pltpu
from jax.sharding import PartitionSpec as P

C = 256
G = 16
CG = C // G
DB = 128
NBLK = 2
ND = DB * NBLK
TILE = 64
TAPS = 17
BLK = 128
RIM = 2
P1 = 6
P2 = 8
PAD = 16
MESH = pl.DeviceIdType.MESH


def window_weights(taps, wide):
    lane = lax.broadcasted_iota(jnp.int32, (G, 4 * BLK), 1)
    group = lax.broadcasted_iota(jnp.int32, (G, 4 * BLK), 0)
    base = jnp.zeros((G, 4 * BLK), jnp.float32)
    for i in range(3):
        for j in range(3):
            pick = (lane == group + (i * wide + j) * G).astype(jnp.float32).astype(jnp.bfloat16)
            base = base + jnp.dot(taps[3 * i + j], pick, preferred_element_type=jnp.float32)
    return base


def weights(sf, ss, w1, w2):
    base = window_weights(sf, P1 + 2)
    for i in range(2):
        for j in range(P1):
            move = (i * (P1 + 2) + j) * G
            piece = pltpu.roll(base, move, 1) if move else base
            at = (i * P1 + j) * G
            w1[at : at + G, :] = piece.astype(jnp.bfloat16)
    base = window_weights(ss, P2 + 2)
    for j in range(P2):
        piece = pltpu.roll(base, j * G, 1) if j else base
        w2[j * G : (j + 1) * G, :] = piece.astype(jnp.bfloat16)
    to = lax.broadcasted_iota(jnp.int32, (P2 * G, P2 * G), 0)
    at = lax.broadcasted_iota(jnp.int32, (P2 * G, P2 * G), 1)
    order = (at == (to % P2) * G + to // P2).astype(jnp.float32).astype(jnp.bfloat16)
    w2[...] = jnp.dot(order, w2[...], preferred_element_type=jnp.float32).astype(jnp.bfloat16)


def correlate(steps, row_of, left, right, act, l32, rt, a_buf, vol, a32):
    strip = left.shape[1] - 2 * PAD
    tiles = strip // BLK
    blocks = right.shape[1] // BLK
    chunk = 32
    chan = lax.broadcasted_iota(jnp.int32, (G, C), 1) // CG
    grp = lax.broadcasted_iota(jnp.int32, (G, C), 0)
    diag = (chan == grp).astype(jnp.float32).astype(jnp.bfloat16)

    def fill(y, x_ext, count, slot):
        for i in range(count):
            row = jnp.broadcast_to(l32[pl.ds(x_ext + (PAD - RIM) + i, 1), :], (G, C)).astype(jnp.bfloat16)
            a_buf[slot + i * G : slot + (i + 1) * G, :] = row * diag

    def emit(y, x_ext, prod, i, xi, scale):
        wide = prod[i * G : (i + 1) * G, :]
        piece = pltpu.roll(wide, wide.shape[1] - 1 - xi, 1)[:, :ND].astype(jnp.bfloat16)
        vol[y, pl.ds(pl.multiple_of((x_ext + i) * G, G), G), :] = piece * scale

    def row_step(step, carry):
        y = row_of(step)
        l32[...] = left[y].astype(jnp.float32)
        for b in range(blocks):
            rt[:, b * BLK : (b + 1) * BLK] = right[y, b * BLK : (b + 1) * BLK, :].T

        for side in range(3):
            a32[side] = act[side, y].astype(jnp.float32)

        def scale_of(side, tile):
            return jnp.broadcast_to(a32[side, pl.ds(tile, 1), :], (G, ND)).astype(jnp.bfloat16)

        def tile_step(t, carry):
            window = rt[:, pl.ds(pl.multiple_of((t + 1) * BLK, BLK), BLK + ND)]
            for half in range(BLK // TILE):
                scale = scale_of(1, t * (BLK // TILE) + half)
                for c in range(TILE // chunk):
                    xi = half * TILE + c * chunk
                    slot = xi * G
                    fill(y, RIM + t * BLK + xi, chunk, slot)
                    prod = jnp.dot(
                        a_buf[slot : slot + chunk * G, :], window, preferred_element_type=jnp.float32
                    )
                    for i in range(chunk):
                        emit(y, RIM + t * BLK + xi, prod, i, xi + i, scale)
            return carry

        lax.fori_loop(0, tiles, tile_step, 0)
        fill(y, 0, RIM, 0)
        prod = jnp.dot(
            a_buf[0 : RIM * G, :], rt[:, 0 : BLK + ND], preferred_element_type=jnp.float32
        )
        scale = scale_of(0, strip // TILE - 1)
        for i in range(RIM):
            emit(y, 0, prod, i, BLK - RIM + i, scale)
        fill(y, RIM + strip, RIM, 0)
        first = (1 + tiles) * BLK
        prod = jnp.dot(
            a_buf[0 : RIM * G, :],
            rt[:, first : first + BLK + ND],
            preferred_element_type=jnp.float32,
        )
        scale = scale_of(2, 0)
        for i in range(RIM):
            emit(y, RIM + strip, prod, i, i, scale)
        return carry

    lax.fori_loop(0, steps, row_step, 0)


def convolve(sides, td, out, vol, h1, h2, w1, w2):
    out_rows, strip, _ = out.shape

    def conv1_window(w):
        at = w * (P1 * G) if isinstance(w, int) else pl.multiple_of(w * (P1 * G), P1 * G)
        for yp in range((out_rows + 2) // 2):
            x = jnp.concatenate(
                [vol[2 * yp + r, pl.ds(at, (P1 + 2) * G), :] for r in range(4)], axis=0
            )
            y = jnp.dot(w1[...], x, preferred_element_type=jnp.float32)
            y = jnp.maximum(y, 0.0).astype(jnp.bfloat16)
            for r in range(2):
                h1[2 * yp + r, pl.ds(at, P1 * G), :] = y[r * P1 * G : (r + 1) * P1 * G, :]

    def conv1_step(q, carry):
        for i in range(3):
            conv1_window(q * 3 + i)
        return carry

    windows = (strip + 2) // P1
    lax.fori_loop(0, windows // 3, conv1_step, 0)
    for w in range(windows // 3 * 3, windows):
        conv1_window(w)

    span = (strip + 2) * G

    @pl.when(jnp.logical_not(sides[0]))
    def _():
        h1[0, 0:span, :] = jnp.zeros((span, ND), jnp.bfloat16)

    @pl.when(jnp.logical_not(sides[1]))
    def _():
        h1[out_rows + 1, 0:span, :] = jnp.zeros((span, ND), jnp.bfloat16)

    @pl.when(jnp.logical_not(sides[2]))
    def _():
        h1[:, 0:G, :] = jnp.zeros((out_rows + 2, G, ND), jnp.bfloat16)

    @pl.when(jnp.logical_not(sides[3]))
    def _():
        h1[:, span - G : span, :] = jnp.zeros((out_rows + 2, G, ND), jnp.bfloat16)

    def conv2_window(w):
        for y in range(out_rows):
            halves = []
            for h in range(2):
                at = pl.multiple_of((w * 2 + h) * (P2 * G), P2 * G)
                x = jnp.concatenate(
                    [h1[y + r, pl.ds(at, (P2 + 2) * G), :] for r in range(3)], axis=0
                )
                r = jnp.dot(w2[:, 0 : 3 * (P2 + 2) * G], x, preferred_element_type=jnp.float32)
                halves.append(jnp.maximum(r, 0.0))
            px = pl.multiple_of(y * strip + w * (2 * P2), 2 * P2)
            for g in range(G):
                both = jnp.concatenate([q[g * P2 : (g + 1) * P2] for q in halves], axis=0)
                h2[g, pl.ds(px, 2 * P2), :] = both.astype(jnp.bfloat16)

    def conv2_step(q, carry):
        for i in range(2):
            conv2_window(q * 2 + i)
        return carry

    lax.fori_loop(0, strip // (4 * P2), conv2_step, 0)

    for y in range(out_rows):
        total = None
        for g in range(G):
            part = jnp.dot(
                h2[g, y * strip : (y + 1) * strip, :], td[g], preferred_element_type=jnp.float32
            )
            total = part if total is None else total + part
        out[y] = total


def kernel(
    dw, left, right, act, sf, ss, out, lx, rx, ax, td, l32, rt, a_buf, vol, h1, h2, w1, w2, a32,
    send, recv, local, row_sem, row_recv,
):
    rows, strip, _ = left.shape
    band, bands = lax.axis_index("rows"), lax.axis_size("rows")
    col, cols = lax.axis_index("cols"), lax.axis_size("cols")
    own = slice(RIM, RIM + rows)
    r0 = BLK + ND
    has_above, has_below = band > 0, band < bands - 1
    has_prev, has_next = col > 0, col < cols - 1

    barrier = pltpu.get_barrier_semaphore()

    def greet(there, device):
        @pl.when(there)
        def _():
            pl.semaphore_signal(barrier, inc=1, device_id=device, device_id_type=MESH)

    greet(has_above, {"rows": band - 1})
    greet(has_below, {"rows": band + 1})
    greet(has_prev, {"cols": col - 1})
    greet(has_next, {"cols": col + 1})
    sides = (has_above, has_below, has_prev, has_next)
    pl.semaphore_wait(barrier, sum(there.astype(jnp.int32) for there in sides))

    halo_rows = []
    for i in range(RIM):
        halo_rows += [RIM - 1 - i, RIM + rows + i]

    def row_copies(device, src, dst, slot):
        one, at = slice(src, src + 1), slice(dst, dst + 1)
        pairs = (
            (left.at[one], lx.at[at, PAD : PAD + strip]),
            (right.at[one], rx.at[at, r0 : r0 + strip]),
            (act.at[one], ax.at[1, at]),
        )
        return [
            pltpu.make_async_remote_copy(
                src_ref=a, dst_ref=b, send_sem=row_sem.at[slot, i], recv_sem=row_recv.at[slot, i],
                device_id=device, device_id_type=MESH,
            )
            for i, (a, b) in enumerate(pairs)
        ]

    def col_copies(forward, part):
        at = own if part == 0 else slice(halo_rows[part - 1], halo_rows[part - 1] + 1)
        if part == 0:
            srcs = (left, right, act)
        else:
            srcs = (
                lx.at[at, PAD : PAD + strip], rx.at[at, r0 : r0 + strip], ax.at[1, at],
            )
        l_src, r_src, a_src = srcs
        if forward:
            pairs = (
                (l_src.at[:, strip - PAD : strip], lx.at[at, 0:PAD]),
                (r_src, rx.at[at, BLK : BLK + strip]),
                (a_src, ax.at[0, at]),
            )
        else:
            pairs = (
                (l_src.at[:, 0:PAD], lx.at[at, PAD + strip : 2 * PAD + strip]),
                (r_src.at[:, 0:PAD], rx.at[at, r0 + strip : r0 + strip + PAD]),
                (a_src, ax.at[2, at]),
            )
        slot = (0 if forward else 1 + 2 * RIM) + part
        device = {"cols": col + 1 if forward else col - 1}
        return [
            pltpu.make_async_remote_copy(
                src_ref=a, dst_ref=b, send_sem=send.at[slot, i], recv_sem=recv.at[slot, i],
                device_id=device, device_id_type=MESH,
            )
            for i, (a, b) in enumerate(pairs)
        ]

    down, up = [], []
    for i in range(RIM):
        down.append(row_copies({"rows": band + 1}, rows - 1 - i, RIM - 1 - i, 2 * i))
        up.append(row_copies({"rows": band - 1}, i, RIM + rows + i, 2 * i + 1))

    def when(there, action):
        @pl.when(there)
        def _():
            action()

    def start(copies):
        for q in copies:
            q.start()

    def got(copies):
        for q in copies:
            q.wait_recv()

    def sent(copies):
        for q in copies:
            q.wait_send()

    for i in range(RIM):
        when(has_below, lambda i=i: start(down[i]))
        when(has_above, lambda i=i: start(up[i]))
    when(has_next, lambda: start(col_copies(True, 0)))
    when(has_prev, lambda: start(col_copies(False, 0)))
    mine = [
        pltpu.make_async_copy(left, lx.at[own, PAD : PAD + strip], local.at[0]),
        pltpu.make_async_copy(right, rx.at[own, r0 : r0 + strip], local.at[1]),
        pltpu.make_async_copy(act, ax.at[1, own], local.at[2]),
    ]
    start(mine)

    def zero(ref):
        ref[...] = jnp.zeros(ref.shape, ref.dtype)

    zero(rx.at[:, 0:BLK])
    zero(rx.at[:, r0 + strip + PAD : r0 + strip + BLK])

    def no_prev():
        zero(lx.at[own, 0:PAD])
        zero(rx.at[own, BLK:r0])
        zero(ax.at[0, own])

    def no_next():
        zero(lx.at[own, PAD + strip : 2 * PAD + strip])
        zero(rx.at[own, r0 + strip : r0 + strip + PAD])
        zero(ax.at[2, own])

    when(jnp.logical_not(has_prev), no_prev)
    when(jnp.logical_not(has_next), no_next)

    def no_rows(first):
        def run():
            at = slice(first, first + RIM)
            zero(lx.at[at])
            zero(rx.at[at, BLK : r0 + strip + PAD])
            for side in range(3):
                zero(ax.at[side, at])
        return run

    def halo_rims(first):
        def run():
            at = slice(first, first + RIM)

            def before():
                zero(lx.at[at, 0:PAD])
                zero(rx.at[at, BLK:r0])
                zero(ax.at[0, at])

            def after():
                zero(lx.at[at, PAD + strip : 2 * PAD + strip])
                zero(rx.at[at, r0 + strip : r0 + strip + PAD])
                zero(ax.at[2, at])

            when(jnp.logical_not(has_prev), before)
            when(jnp.logical_not(has_next), after)
        return run

    for there, first in ((has_above, 0), (has_below, RIM + rows)):
        when(jnp.logical_not(there), no_rows(first))
        when(there, halo_rims(first))

    def band_steps(lane, first, last):
        def step(e, carry):
            at = e * PAD
            place = (
                ND - 1 + TAPS // 2 - lane - at
                - lax.broadcasted_iota(jnp.int32, (PAD, BLK), 0)
                - lax.broadcasted_iota(jnp.int32, (PAD, BLK), 1)
            )
            for g in range(G):
                total = jnp.zeros((PAD, BLK), jnp.float32)
                for k in range(TAPS):
                    total = jnp.where(place == k, dw[k, g], total)
                td[g, pl.ds(pl.multiple_of(at, PAD), PAD), lane : lane + BLK] = total.astype(
                    jnp.bfloat16
                )
            return carry

        lax.fori_loop(first, last, step, 0)

    half = BLK // PAD
    td[:, 0 : BLK - PAD, 0:BLK] = jnp.zeros((G, BLK - PAD, BLK), jnp.bfloat16)
    td[:, BLK + PAD : ND, BLK:ND] = jnp.zeros((G, BLK - PAD, BLK), jnp.bfloat16)
    band_steps(0, half - 1, 2 * half)
    band_steps(BLK, 0, half + 1)

    weights(sf, ss, w1, w2)

    def arrived(part):
        when(has_prev, lambda: got(col_copies(True, part)))
        when(has_next, lambda: got(col_copies(False, part)))

    def left_off(part):
        when(has_next, lambda: sent(col_copies(True, part)))
        when(has_prev, lambda: sent(col_copies(False, part)))

    for q in mine:
        q.wait()
    arrived(0)
    work = (lx, rx, ax, l32, rt, a_buf, vol, a32)
    correlate(rows, lambda i: i + RIM, *work)

    for i in range(RIM):
        halves = ((has_above, down[i], 2 * i + 1), (has_below, up[i], 2 * i + 2))
        for there, copies, part in halves:
            def forward(copies=copies, part=part):
                got(copies)
                when(has_next, lambda: start(col_copies(True, part)))
                when(has_prev, lambda: start(col_copies(False, part)))
            when(there, forward)
        for there, copies, part in halves:
            when(there, lambda part=part: arrived(part))
        near, far = halo_rows[2 * i], halo_rows[2 * i + 1]
        correlate(2, lambda j, near=near, far=far: near + j * (far - near), *work)

    left_off(0)
    for i in range(RIM):
        when(has_below, lambda i=i: sent(down[i]))
        when(has_above, lambda i=i: sent(up[i]))
        when(has_above, lambda i=i: left_off(2 * i + 1))
        when(has_below, lambda i=i: left_off(2 * i + 2))
    convolve(sides, td, out, vol, h1, h2, w1, w2)


def body(
    left_feat, right_feat, block_list, block_count, spatial_first, spatial_second, disparity_weight
):
    rows, strip, _ = left_feat.shape
    if strip != ND or lax.axis_size("cols") > 2 or rows != RIM:
        raise ValueError("unsupported strip")
    tiles = strip // TILE
    n = rows + 2 * RIM

    live = jnp.arange(block_list.shape[2], dtype=jnp.int32) < block_count[0][:, None]
    lane_block = NBLK - 1 - jnp.arange(ND, dtype=jnp.int32) // DB
    hits = (block_list[0][:, :, None] == lane_block[None, None, :]) & live[:, :, None]
    act = jnp.where(jnp.any(hits, axis=1), CG ** (-0.5), 0.0).astype(jnp.bfloat16)
    act = jnp.broadcast_to(jnp.pad(act, ((0, PAD - tiles), (0, 0)))[None], (rows, PAD, ND))

    vmem = pl.BlockSpec(memory_space=pltpu.VMEM)
    smem = pl.BlockSpec(memory_space=pltpu.SMEM)
    right_len = BLK + ND + strip + BLK
    return pl.pallas_call(
        kernel,
        out_shape=jax.ShapeDtypeStruct((rows, strip, ND), jnp.float32),
        in_specs=[smem] + [vmem] * 5,
        out_specs=vmem,
        scratch_shapes=[
            pltpu.VMEM((n, strip + 2 * PAD, C), jnp.bfloat16),
            pltpu.VMEM((n, right_len, C), jnp.bfloat16),
            pltpu.VMEM((3, n, PAD, ND), jnp.bfloat16),
            pltpu.VMEM((G, ND, ND), jnp.bfloat16),
            pltpu.VMEM((strip + 2 * PAD, C), jnp.float32),
            pltpu.VMEM((C, right_len), jnp.bfloat16),
            pltpu.VMEM((BLK * G, C), jnp.bfloat16),
            pltpu.VMEM((n, (strip + 2 * RIM) * G, ND), jnp.bfloat16),
            pltpu.VMEM((rows + 2, (strip + 2) * G, ND), jnp.bfloat16),
            pltpu.VMEM((G, rows * strip, ND), jnp.bfloat16),
            pltpu.VMEM((2 * P1 * G, 4 * BLK), jnp.bfloat16),
            pltpu.VMEM((P2 * G, 4 * BLK), jnp.bfloat16),
            pltpu.VMEM((3, PAD, ND), jnp.float32),
            pltpu.SemaphoreType.DMA((2 + 4 * RIM, 3)),
            pltpu.SemaphoreType.DMA((2 + 4 * RIM, 3)),
            pltpu.SemaphoreType.DMA((3,)),
            pltpu.SemaphoreType.DMA((2 * RIM, 3)),
            pltpu.SemaphoreType.DMA((2 * RIM, 3)),
        ],
        compiler_params=pltpu.CompilerParams(
            collective_id=0, has_side_effects=True, vmem_limit_bytes=56 * 1024 * 1024
        ),
        name="cost_volume",
    )(
        disparity_weight.astype(jnp.float32), left_feat, right_feat, act,
        spatial_first.reshape(9, G, G), spatial_second.reshape(9, G, G),
    )


def solution(mesh):
    in_specs = (
        P(("pairs", "rows"), "cols", None),
        P(("pairs", "rows"), "cols", None),
        P(("pairs", "rows"), "cols", None),
        P(("pairs", "rows"), "cols"),
        P(),
        P(),
        P(),
    )
    out_specs = P(("pairs", "rows"), "cols", None)
    return jax.shard_map(body, mesh=mesh, in_specs=in_specs, out_specs=out_specs, check_vma=False)
```

```python
import jax
import jax.numpy as jnp
from jax import lax
from jax.experimental import pallas as pl
from jax.experimental.pallas import tpu as pltpu
from jax.sharding import PartitionSpec as P

C = 256
G = 16
CG = C // G
DB = 128
NBLK = 2
ND = DB * NBLK
TILE = 64
TAPS = 17
BLK = 128
RIM = 2
P1 = 6
P2 = 8
PAD = 16
MESH = pl.DeviceIdType.MESH


def window_weights(taps, wide):
    lane = lax.broadcasted_iota(jnp.int32, (G, 4 * BLK), 1)
    group = lax.broadcasted_iota(jnp.int32, (G, 4 * BLK), 0)
    base = jnp.zeros((G, 4 * BLK), jnp.float32)
    for i in range(3):
        for j in range(3):
            pick = (lane == group + (i * wide + j) * G).astype(jnp.float32).astype(jnp.bfloat16)
            base = base + jnp.dot(taps[3 * i + j], pick, preferred_element_type=jnp.float32)
    return base


def weights(sf, ss, w1, w2):
    base = window_weights(sf, P1 + 2)
    for i in range(2):
        for j in range(P1):
            move = (i * (P1 + 2) + j) * G
            piece = pltpu.roll(base, move, 1) if move else base
            at = (i * P1 + j) * G
            w1[at : at + G, :] = piece.astype(jnp.bfloat16)
    base = window_weights(ss, P2 + 2)
    for j in range(P2):
        piece = pltpu.roll(base, j * G, 1) if j else base
        w2[j * G : (j + 1) * G, :] = piece.astype(jnp.bfloat16)
    to = lax.broadcasted_iota(jnp.int32, (P2 * G, P2 * G), 0)
    at = lax.broadcasted_iota(jnp.int32, (P2 * G, P2 * G), 1)
    order = (at == (to % P2) * G + to // P2).astype(jnp.float32).astype(jnp.bfloat16)
    w2[...] = jnp.dot(order, w2[...], preferred_element_type=jnp.float32).astype(jnp.bfloat16)


def correlate(steps, row_of, left, right, act, l32, rt, a_buf, vol, a32):
    strip = left.shape[1] - 2 * PAD
    tiles = strip // BLK
    blocks = right.shape[1] // BLK
    chunk = 64
    chan = lax.broadcasted_iota(jnp.int32, (G, C), 1) // CG
    grp = lax.broadcasted_iota(jnp.int32, (G, C), 0)
    diag = (chan == grp).astype(jnp.float32).astype(jnp.bfloat16)

    def fill(y, x_ext, count, slot):
        for i in range(count):
            row = jnp.broadcast_to(l32[pl.ds(x_ext + (PAD - RIM) + i, 1), :], (G, C)).astype(jnp.bfloat16)
            a_buf[slot + i * G : slot + (i + 1) * G, :] = row * diag

    def emit(y, x_ext, prod, i, xi, scale):
        wide = prod[i * G : (i + 1) * G, :]
        piece = pltpu.roll(wide, wide.shape[1] - 1 - xi, 1)[:, :ND].astype(jnp.bfloat16)
        vol[y, pl.ds(pl.multiple_of((x_ext + i) * G, G), G), :] = piece * scale

    def row_step(step, carry):
        y = row_of(step)
        l32[...] = left[y].astype(jnp.float32)
        for b in range(blocks):
            rt[:, b * BLK : (b + 1) * BLK] = right[y, b * BLK : (b + 1) * BLK, :].T

        for side in range(3):
            a32[side] = act[side, y].astype(jnp.float32)

        def scale_of(side, tile):
            return jnp.broadcast_to(a32[side, pl.ds(tile, 1), :], (G, ND)).astype(jnp.bfloat16)

        def tile_step(t, carry):
            window = rt[:, pl.ds(pl.multiple_of((t + 1) * BLK, BLK), BLK + ND)]
            for half in range(BLK // TILE):
                scale = scale_of(1, t * (BLK // TILE) + half)
                for c in range(TILE // chunk):
                    xi = half * TILE + c * chunk
                    slot = xi * G
                    fill(y, RIM + t * BLK + xi, chunk, slot)
                    prod = jnp.dot(
                        a_buf[slot : slot + chunk * G, :], window, preferred_element_type=jnp.float32
                    )
                    for i in range(chunk):
                        emit(y, RIM + t * BLK + xi, prod, i, xi + i, scale)
            return carry

        lax.fori_loop(0, tiles, tile_step, 0)
        fill(y, 0, RIM, 0)
        prod = jnp.dot(
            a_buf[0 : RIM * G, :], rt[:, 0 : BLK + ND], preferred_element_type=jnp.float32
        )
        scale = scale_of(0, strip // TILE - 1)
        for i in range(RIM):
            emit(y, 0, prod, i, BLK - RIM + i, scale)
        fill(y, RIM + strip, RIM, 0)
        first = (1 + tiles) * BLK
        prod = jnp.dot(
            a_buf[0 : RIM * G, :],
            rt[:, first : first + BLK + ND],
            preferred_element_type=jnp.float32,
        )
        scale = scale_of(2, 0)
        for i in range(RIM):
            emit(y, RIM + strip, prod, i, i, scale)
        return carry

    lax.fori_loop(0, steps, row_step, 0)


def convolve(sides, td, out, vol, h1, h2, w1, w2):
    out_rows, strip, _ = out.shape

    def conv1_window(w):
        at = w * (P1 * G) if isinstance(w, int) else pl.multiple_of(w * (P1 * G), P1 * G)
        for yp in range((out_rows + 2) // 2):
            x = jnp.concatenate(
                [vol[2 * yp + r, pl.ds(at, (P1 + 2) * G), :] for r in range(4)], axis=0
            )
            y = jnp.dot(w1[...], x, preferred_element_type=jnp.float32)
            y = jnp.maximum(y, 0.0).astype(jnp.bfloat16)
            for r in range(2):
                h1[2 * yp + r, pl.ds(at, P1 * G), :] = y[r * P1 * G : (r + 1) * P1 * G, :]

    def conv1_step(q, carry):
        for i in range(3):
            conv1_window(q * 3 + i)
        return carry

    windows = (strip + 2) // P1
    lax.fori_loop(0, windows // 3, conv1_step, 0)
    for w in range(windows // 3 * 3, windows):
        conv1_window(w)

    span = (strip + 2) * G

    @pl.when(jnp.logical_not(sides[0]))
    def _():
        h1[0, 0:span, :] = jnp.zeros((span, ND), jnp.bfloat16)

    @pl.when(jnp.logical_not(sides[1]))
    def _():
        h1[out_rows + 1, 0:span, :] = jnp.zeros((span, ND), jnp.bfloat16)

    @pl.when(jnp.logical_not(sides[2]))
    def _():
        h1[:, 0:G, :] = jnp.zeros((out_rows + 2, G, ND), jnp.bfloat16)

    @pl.when(jnp.logical_not(sides[3]))
    def _():
        h1[:, span - G : span, :] = jnp.zeros((out_rows + 2, G, ND), jnp.bfloat16)

    def conv2_window(w):
        for y in range(out_rows):
            halves = []
            for h in range(2):
                at = pl.multiple_of((w * 2 + h) * (P2 * G), P2 * G)
                x = jnp.concatenate(
                    [h1[y + r, pl.ds(at, (P2 + 2) * G), :] for r in range(3)], axis=0
                )
                r = jnp.dot(w2[:, 0 : 3 * (P2 + 2) * G], x, preferred_element_type=jnp.float32)
                halves.append(jnp.maximum(r, 0.0))
            px = pl.multiple_of(y * strip + w * (2 * P2), 2 * P2)
            for g in range(G):
                both = jnp.concatenate([q[g * P2 : (g + 1) * P2] for q in halves], axis=0)
                h2[g, pl.ds(px, 2 * P2), :] = both.astype(jnp.bfloat16)

    def conv2_step(q, carry):
        for i in range(2):
            conv2_window(q * 2 + i)
        return carry

    lax.fori_loop(0, strip // (4 * P2), conv2_step, 0)

    for y in range(out_rows):
        total = None
        for g in range(G):
            part = jnp.dot(
                h2[g, y * strip : (y + 1) * strip, :], td[g], preferred_element_type=jnp.float32
            )
            total = part if total is None else total + part
        out[y] = total


def kernel(
    dw, left, right, act, sf, ss, out, lx, rx, ax, td, l32, rt, a_buf, vol, h1, h2, w1, w2, a32,
    send, recv, local, row_sem, row_recv,
):
    rows, strip, _ = left.shape
    band, bands = lax.axis_index("rows"), lax.axis_size("rows")
    col, cols = lax.axis_index("cols"), lax.axis_size("cols")
    own = slice(RIM, RIM + rows)
    r0 = BLK + ND
    has_above, has_below = band > 0, band < bands - 1
    has_prev, has_next = col > 0, col < cols - 1

    barrier = pltpu.get_barrier_semaphore()

    def greet(there, device):
        @pl.when(there)
        def _():
            pl.semaphore_signal(barrier, inc=1, device_id=device, device_id_type=MESH)

    greet(has_above, {"rows": band - 1})
    greet(has_below, {"rows": band + 1})
    greet(has_prev, {"cols": col - 1})
    greet(has_next, {"cols": col + 1})
    sides = (has_above, has_below, has_prev, has_next)
    pl.semaphore_wait(barrier, sum(there.astype(jnp.int32) for there in sides))

    halo_rows = []
    for i in range(RIM):
        halo_rows += [RIM - 1 - i, RIM + rows + i]

    def row_copies(device, src, dst, slot):
        one, at = slice(src, src + 1), slice(dst, dst + 1)
        pairs = (
            (left.at[one], lx.at[at, PAD : PAD + strip]),
            (right.at[one], rx.at[at, r0 : r0 + strip]),
            (act.at[one], ax.at[1, at]),
        )
        return [
            pltpu.make_async_remote_copy(
                src_ref=a, dst_ref=b, send_sem=row_sem.at[slot, i], recv_sem=row_recv.at[slot, i],
                device_id=device, device_id_type=MESH,
            )
            for i, (a, b) in enumerate(pairs)
        ]

    def col_copies(forward, part):
        at = own if part == 0 else slice(halo_rows[part - 1], halo_rows[part - 1] + 1)
        if part == 0:
            srcs = (left, right, act)
        else:
            srcs = (
                lx.at[at, PAD : PAD + strip], rx.at[at, r0 : r0 + strip], ax.at[1, at],
            )
        l_src, r_src, a_src = srcs
        if forward:
            pairs = (
                (l_src.at[:, strip - PAD : strip], lx.at[at, 0:PAD]),
                (r_src, rx.at[at, BLK : BLK + strip]),
                (a_src, ax.at[0, at]),
            )
        else:
            pairs = (
                (l_src.at[:, 0:PAD], lx.at[at, PAD + strip : 2 * PAD + strip]),
                (r_src.at[:, 0:PAD], rx.at[at, r0 + strip : r0 + strip + PAD]),
                (a_src, ax.at[2, at]),
            )
        slot = (0 if forward else 1 + 2 * RIM) + part
        device = {"cols": col + 1 if forward else col - 1}
        return [
            pltpu.make_async_remote_copy(
                src_ref=a, dst_ref=b, send_sem=send.at[slot, i], recv_sem=recv.at[slot, i],
                device_id=device, device_id_type=MESH,
            )
            for i, (a, b) in enumerate(pairs)
        ]

    down, up = [], []
    for i in range(RIM):
        down.append(row_copies({"rows": band + 1}, rows - 1 - i, RIM - 1 - i, 2 * i))
        up.append(row_copies({"rows": band - 1}, i, RIM + rows + i, 2 * i + 1))

    def when(there, action):
        @pl.when(there)
        def _():
            action()

    def start(copies):
        for q in copies:
            q.start()

    def got(copies):
        for q in copies:
            q.wait_recv()

    def sent(copies):
        for q in copies:
            q.wait_send()

    for i in range(RIM):
        when(has_below, lambda i=i: start(down[i]))
        when(has_above, lambda i=i: start(up[i]))
    when(has_next, lambda: start(col_copies(True, 0)))
    when(has_prev, lambda: start(col_copies(False, 0)))
    mine = [
        pltpu.make_async_copy(left, lx.at[own, PAD : PAD + strip], local.at[0]),
        pltpu.make_async_copy(right, rx.at[own, r0 : r0 + strip], local.at[1]),
        pltpu.make_async_copy(act, ax.at[1, own], local.at[2]),
    ]
    start(mine)

    def zero(ref):
        ref[...] = jnp.zeros(ref.shape, ref.dtype)

    zero(rx.at[:, 0:BLK])
    zero(rx.at[:, r0 + strip + PAD : r0 + strip + BLK])

    def no_prev():
        zero(lx.at[own, 0:PAD])
        zero(rx.at[own, BLK:r0])
        zero(ax.at[0, own])

    def no_next():
        zero(lx.at[own, PAD + strip : 2 * PAD + strip])
        zero(rx.at[own, r0 + strip : r0 + strip + PAD])
        zero(ax.at[2, own])

    when(jnp.logical_not(has_prev), no_prev)
    when(jnp.logical_not(has_next), no_next)

    def no_rows(first):
        def run():
            at = slice(first, first + RIM)
            zero(lx.at[at])
            zero(rx.at[at, BLK : r0 + strip + PAD])
            for side in range(3):
                zero(ax.at[side, at])
        return run

    def halo_rims(first):
        def run():
            at = slice(first, first + RIM)

            def before():
                zero(lx.at[at, 0:PAD])
                zero(rx.at[at, BLK:r0])
                zero(ax.at[0, at])

            def after():
                zero(lx.at[at, PAD + strip : 2 * PAD + strip])
                zero(rx.at[at, r0 + strip : r0 + strip + PAD])
                zero(ax.at[2, at])

            when(jnp.logical_not(has_prev), before)
            when(jnp.logical_not(has_next), after)
        return run

    for there, first in ((has_above, 0), (has_below, RIM + rows)):
        when(jnp.logical_not(there), no_rows(first))
        when(there, halo_rims(first))

    def band_steps(lane, first, last):
        def step(e, carry):
            at = e * PAD
            place = (
                ND - 1 + TAPS // 2 - lane - at
                - lax.broadcasted_iota(jnp.int32, (PAD, BLK), 0)
                - lax.broadcasted_iota(jnp.int32, (PAD, BLK), 1)
            )
            for g in range(G):
                total = jnp.zeros((PAD, BLK), jnp.float32)
                for k in range(TAPS):
                    total = jnp.where(place == k, dw[k, g], total)
                td[g, pl.ds(pl.multiple_of(at, PAD), PAD), lane : lane + BLK] = total.astype(
                    jnp.bfloat16
                )
            return carry

        lax.fori_loop(first, last, step, 0)

    half = BLK // PAD
    td[:, 0 : BLK - PAD, 0:BLK] = jnp.zeros((G, BLK - PAD, BLK), jnp.bfloat16)
    td[:, BLK + PAD : ND, BLK:ND] = jnp.zeros((G, BLK - PAD, BLK), jnp.bfloat16)
    band_steps(0, half - 1, 2 * half)
    band_steps(BLK, 0, half + 1)

    weights(sf, ss, w1, w2)

    def arrived(part):
        when(has_prev, lambda: got(col_copies(True, part)))
        when(has_next, lambda: got(col_copies(False, part)))

    def left_off(part):
        when(has_next, lambda: sent(col_copies(True, part)))
        when(has_prev, lambda: sent(col_copies(False, part)))

    for q in mine:
        q.wait()
    arrived(0)
    work = (lx, rx, ax, l32, rt, a_buf, vol, a32)
    correlate(rows, lambda i: i + RIM, *work)

    for i in range(RIM):
        halves = ((has_above, down[i], 2 * i + 1), (has_below, up[i], 2 * i + 2))
        for there, copies, part in halves:
            def forward(copies=copies, part=part):
                got(copies)
                when(has_next, lambda: start(col_copies(True, part)))
                when(has_prev, lambda: start(col_copies(False, part)))
            when(there, forward)
        for there, copies, part in halves:
            when(there, lambda part=part: arrived(part))
        near, far = halo_rows[2 * i], halo_rows[2 * i + 1]
        correlate(2, lambda j, near=near, far=far: near + j * (far - near), *work)

    left_off(0)
    for i in range(RIM):
        when(has_below, lambda i=i: sent(down[i]))
        when(has_above, lambda i=i: sent(up[i]))
        when(has_above, lambda i=i: left_off(2 * i + 1))
        when(has_below, lambda i=i: left_off(2 * i + 2))
    convolve(sides, td, out, vol, h1, h2, w1, w2)


def body(
    left_feat, right_feat, block_list, block_count, spatial_first, spatial_second, disparity_weight
):
    rows, strip, _ = left_feat.shape
    if strip != ND or lax.axis_size("cols") > 2 or rows != RIM:
        raise ValueError("unsupported strip")
    tiles = strip // TILE
    n = rows + 2 * RIM

    live = jnp.arange(block_list.shape[2], dtype=jnp.int32) < block_count[0][:, None]
    lane_block = NBLK - 1 - jnp.arange(ND, dtype=jnp.int32) // DB
    hits = (block_list[0][:, :, None] == lane_block[None, None, :]) & live[:, :, None]
    act = jnp.where(jnp.any(hits, axis=1), CG ** (-0.5), 0.0).astype(jnp.bfloat16)
    act = jnp.broadcast_to(jnp.pad(act, ((0, PAD - tiles), (0, 0)))[None], (rows, PAD, ND))

    vmem = pl.BlockSpec(memory_space=pltpu.VMEM)
    smem = pl.BlockSpec(memory_space=pltpu.SMEM)
    right_len = BLK + ND + strip + BLK
    return pl.pallas_call(
        kernel,
        out_shape=jax.ShapeDtypeStruct((rows, strip, ND), jnp.float32),
        in_specs=[smem] + [vmem] * 5,
        out_specs=vmem,
        scratch_shapes=[
            pltpu.VMEM((n, strip + 2 * PAD, C), jnp.bfloat16),
            pltpu.VMEM((n, right_len, C), jnp.bfloat16),
            pltpu.VMEM((3, n, PAD, ND), jnp.bfloat16),
            pltpu.VMEM((G, ND, ND), jnp.bfloat16),
            pltpu.VMEM((strip + 2 * PAD, C), jnp.float32),
            pltpu.VMEM((C, right_len), jnp.bfloat16),
            pltpu.VMEM((BLK * G, C), jnp.bfloat16),
            pltpu.VMEM((n, (strip + 2 * RIM) * G, ND), jnp.bfloat16),
            pltpu.VMEM((rows + 2, (strip + 2) * G, ND), jnp.bfloat16),
            pltpu.VMEM((G, rows * strip, ND), jnp.bfloat16),
            pltpu.VMEM((2 * P1 * G, 4 * BLK), jnp.bfloat16),
            pltpu.VMEM((P2 * G, 4 * BLK), jnp.bfloat16),
            pltpu.VMEM((3, PAD, ND), jnp.float32),
            pltpu.SemaphoreType.DMA((2 + 4 * RIM, 3)),
            pltpu.SemaphoreType.DMA((2 + 4 * RIM, 3)),
            pltpu.SemaphoreType.DMA((3,)),
            pltpu.SemaphoreType.DMA((2 * RIM, 3)),
            pltpu.SemaphoreType.DMA((2 * RIM, 3)),
        ],
        compiler_params=pltpu.CompilerParams(
            collective_id=0, has_side_effects=True, vmem_limit_bytes=56 * 1024 * 1024
        ),
        name="cost_volume",
    )(
        disparity_weight.astype(jnp.float32), left_feat, right_feat, act,
        spatial_first.reshape(9, G, G), spatial_second.reshape(9, G, G),
    )


def solution(mesh):
    in_specs = (
        P(("pairs", "rows"), "cols", None),
        P(("pairs", "rows"), "cols", None),
        P(("pairs", "rows"), "cols", None),
        P(("pairs", "rows"), "cols"),
        P(),
        P(),
        P(),
    )
    out_specs = P(("pairs", "rows"), "cols", None)
    return jax.shard_map(body, mesh=mesh, in_specs=in_specs, out_specs=out_specs, check_vma=False)
```
